256 devices in a mesh: atoms: 32 (over x, z_lo, core), blk: 8 (over z_hi, y).
Axes of the slice: x: 4, y: 4, z: 8 (z_hi: 2, z_lo: 4; z = z_hi * 4 + z_lo), core: 2. Of those that a mesh axis runs over, the one named last changes fastest.
Arguments:
- desc: bfloat16 [524288, 768], P(('atoms', 'blk')), may hold values from -6 to 6
- species: int32 [524288], P(('atoms', 'blk')), may hold values from 0 to 1
- atom_cfg: int32 [524288], P(('atoms', 'blk')), may hold values from 0 to 255
- slot: int32 [256], replicated, may hold values from 0 to 255, each once
- weights: float32 [256], P('atoms'), may hold values from 0.25 to 4
Outputs:
- normal_matrix: float32 [1536, 1536], P('blk')
- config_rows: float32 [256, 1536], P('atoms', 'blk')
The draws below stay inside these ranges and needn't reach their ends.
All inputs are finite; a program needn't handle non-finite values.
Results may differ from the reference program's by a relative error of at most 0.0003.
Values sent between devices are 32-bit elements; how exact they have to be, the bound alone decides.
No kernel may reach another device: no remote copies, remote signals or barrier semaphores. Data moves between devices by JAX's collectives and lax.ppermute only.
A program may use at most 64 MiB of HBM per device.

```python
import math
import jax
import jax.numpy as jnp
import numpy as np
from jax import lax

DESC = 768
ATOM_DEV = 2048
COLS = 1536
CONFIGS = 256
ATOMS = 524288
NORM_ROWS = 65536


def plant(array, key, low, high):
    spot = [jax.random.randint(jax.random.fold_in(key, axis), (), 0, length) for axis, length in enumerate(array.shape)]
    longest = array.shape.index(max(array.shape))
    beside = spot[:longest] + [(spot[longest] + 1) % array.shape[longest]] + spot[longest + 1:]
    return array.at[tuple(spot)].set(low).at[tuple(beside)].set(high)


def block_scale(stream_key, extent, split, smallest, high):
    gain, own = 1.0, jax.random.fold_in(stream_key, 6)
    for dim, blocks in split:
        steps = jnp.exp(jax.random.uniform(jax.random.fold_in(own, dim), (blocks,), jnp.float32, smallest / len(split), high / len(split)))
        gain = gain * jnp.repeat(steps, extent[dim] // blocks).reshape([-1 if axis == dim else 1 for axis in range(len(extent))])
    return gain


def rank_table(amount, lean):
    loads = [(1 << 20) // math.isqrt(rank ** lean) + 1 for rank in range(1, amount + 1)]
    scale = 1 + sum(loads) // (1 << 30)
    return np.cumsum(np.array([max(1, weight // scale) for weight in loads]))


def ranked_ids(rng, shape, amount, slope):
    grid = rank_table(amount, slope)
    lot = jax.random.randint(jax.random.fold_in(rng, 1), shape, 0, int(grid[amount - 1]))
    standing = jnp.searchsorted(jnp.asarray(grid, jnp.int32), lot, side="right")
    return jax.random.permutation(jax.random.fold_in(rng, 2), amount)[standing].astype(jnp.int32)


def normal_values(rng, shape, width, most, pieces=(), kind=jnp.bfloat16):
    values = width * jax.random.normal(rng, shape, jnp.float32)
    if pieces:
        values = values * block_scale(rng, shape, pieces, -0.22, 0.18)
    return jnp.clip(values, -most, most).astype(kind)


def setup_inputs(seed: int = 0) -> dict:
    key_of = jax.random.split(jax.random.key(seed), 6)
    return {
        "desc": normal_values(key_of[0], (ATOMS, DESC), 1.0, 6.0, ((0, 256),)),
        "species": plant(jax.random.randint(key_of[1], (ATOMS,), 0, 2), jax.random.fold_in(key_of[1], 1), 0, 1).astype(jnp.int32),
        "atom_cfg": plant(ranked_ids(key_of[2], (ATOMS,), CONFIGS, 2), jax.random.fold_in(key_of[2], 3), 0, CONFIGS - 1).astype(jnp.int32),
        "slot": jax.random.permutation(key_of[3], CONFIGS).astype(jnp.int32),
        "weights": jnp.clip(jnp.exp(math.log(4.0) - 2.7725887 * jax.random.uniform(key_of[4], (CONFIGS,), jnp.float32) ** block_scale(key_of[4], (CONFIGS,), ((0, 32),), -0.2, 0.2)), 0.25, 4.0),
    }


def reference(desc, species, atom_cfg, slot, weights):
    slot_of = jnp.take(slot, atom_cfg).astype(jnp.int32)
    keys = slot_of * 2 + species
    blocks = ATOMS // ATOM_DEV
    desc_blocks = desc.reshape(blocks, ATOM_DEV, DESC)
    key_blocks = keys.reshape(blocks, ATOM_DEV)
    spec_blocks = species.reshape(blocks, ATOM_DEV)

    def step(carry, item):
        sums, gram = carry
        block_desc, block_keys, block_spec = item
        values = block_desc.astype(jnp.float32)
        sums = sums + jax.ops.segment_sum(values, block_keys, num_segments=2 * CONFIGS)
        first = (block_spec == 0).astype(jnp.float32)[:, None]
        gram_first = jnp.dot((values * first).T, values, precision=lax.Precision.HIGHEST)
        gram_second = jnp.dot((values * (1.0 - first)).T, values, precision=lax.Precision.HIGHEST)
        return ((sums, gram + jnp.stack([gram_first, gram_second])), None)
    start = (jnp.zeros((2 * CONFIGS, DESC), jnp.float32), jnp.zeros((2, DESC, DESC), jnp.float32))
    (sums, gram), _ = lax.scan(step, start, (desc_blocks, key_blocks, spec_blocks))
    scale = 1.0 / math.sqrt(ATOMS / CONFIGS)
    config_rows = sums.reshape(CONFIGS, COLS) * scale
    cfg_gram = jnp.dot((config_rows * weights[:, None]).T, config_rows, precision=lax.Precision.HIGHEST) / CONFIGS
    zeros = jnp.zeros((DESC, DESC), jnp.float32)
    atom_gram = jnp.concatenate([jnp.concatenate([gram[0], zeros], 1), jnp.concatenate([zeros, gram[1]], 1)], 0)
    normal_matrix = cfg_gram + atom_gram / NORM_ROWS
    return (normal_matrix, config_rows)
```

```python
import math

import jax
import jax.numpy as jnp
from jax import lax
from jax.experimental import pallas as pl
from jax.experimental.pallas import tpu as pltpu
from jax.sharding import Mesh, PartitionSpec as P

AXES = ("x", "l", "c", "h", "y")
SIZES = (4, 4, 2, 2, 4)
TILE = 256
OFF = ((0, 1), (0, 2), (1, 2))
VMEM_LIMIT = 56 << 20


def local_kernel(core_ref, desc_ref, species_ref, cfg_ref, slot_ref, keep_ref, send_ref, turned):
    core = core_ref[0]
    atoms, width = desc_ref.shape
    configs = slot_ref.shape[1]
    turned[...] = desc_ref[...].T
    species = species_ref[...]
    ids = lax.broadcasted_iota(jnp.int32, (configs, atoms), 0)
    member = (cfg_ref[...] == ids).astype(jnp.bfloat16)
    rows = lax.broadcasted_iota(jnp.int32, (configs, configs), 0)
    place = (slot_ref[...] == rows).astype(jnp.bfloat16)
    placed = jnp.dot(place, member, preferred_element_type=jnp.float32).astype(jnp.bfloat16)

    def put(first, second, start, size):
        keep_ref[:, start : start + size, :] = jnp.where(core == 0, first, second)
        send_ref[:, start : start + size, :] = jnp.where(core == 0, second, first)

    for kind in range(2):
        mask = (species == kind).astype(jnp.bfloat16)
        sums = jnp.dot(placed * mask, desc_ref[...], preferred_element_type=jnp.float32)
        for j in range(3):
            tile = sums[:, j * TILE : (j + 1) * TILE].reshape(16, 2, 8, TILE)
            put(tile[:, 0], tile[:, 1], 96 + (kind * 3 + j) * 8, 8)
        tiles = {}
        for i in range(3):
            left = turned[i * TILE : (i + 1) * TILE, :] * mask
            for j in range(i, 3):
                tiles[i, j] = jnp.dot(
                    left, desc_ref[:, j * TILE : (j + 1) * TILE], preferred_element_type=jnp.float32
                ).reshape(16, 16, TILE)
        for b in range(3):
            put(tiles[OFF[b]], tiles[b, b], (kind * 3 + b) * 16, 16)


def add_kernel(a_ref, b_ref, out_ref):
    out_ref[...] = a_ref[...] + b_ref[...]


def plane_kernel(got_ref, out_ref):
    total = got_ref[0]
    for k in range(1, got_ref.shape[0]):
        total = total + got_ref[k]
    for k in range(out_ref.shape[0]):
        half = k % 2
        out_ref[k, :48, :] = total[half * 48 : half * 48 + 48]
        out_ref[k, 48:, :] = total[96:]


def spread_kernel(scale, got_ref, root_ref, out_ref):
    total = got_ref[0]
    for k in range(1, got_ref.shape[0]):
        total = total + got_ref[k]
    gram = total[:48]
    factor = jnp.tile(root_ref[:, :1] * scale, (6, 1))
    rows = total[48:] * factor
    for k in range(out_ref.shape[0]):
        out_ref[k, :48, :] = gram
        out_ref[k, 48:, :] = rows


def final_kernel(norm, pos_ref, mine_ref, other_ref, root_ref, normal_ref, cfg_ref, full, left, gram):
    core, kind, part, owner = pos_ref[0], pos_ref[1], pos_ref[2], pos_ref[3]
    width = gram.shape[1]
    band = left.shape[1]

    def half(which, start, size):
        a = mine_ref[:, start : start + size, :]
        b = other_ref[:, start : start + size, :]
        return jnp.where(core == which, a, b)

    for j in range(6):
        pair = [half(which, 48 + 8 * j, 8)[:, None] for which in range(2)]
        full[:, j * TILE : (j + 1) * TILE] = jnp.concatenate(pair, 1).reshape(256, TILE)

    def off(b):
        return half(0, 16 * b, 16).reshape(TILE, TILE)

    def diag(b):
        return half(1, 16 * b, 16).reshape(TILE, TILE)

    def block(i, j, lo, hi):
        if i == j:
            return diag(i)[lo:hi]
        if i < j:
            return off(OFF.index((i, j)))[lo:hi]
        return off(OFF.index((j, i)))[:, lo:hi].T

    for k in range(4):

        @pl.when(part == k)
        def _():
            cols = slice(k * band, (k + 1) * band)
            shifted = slice(width + k * band, width + (k + 1) * band)
            left[...] = jnp.where(kind == 0, full[:, cols], full[:, shifted])
            own = pl.ds(pl.multiple_of(owner * 8, 8), 8)
            tile = jnp.where(kind == 0, full[own, cols], full[own, shifted])
            cfg_ref[...] = tile / root_ref[:, :1]
            at = k * band
            while at < (k + 1) * band:
                i = at // TILE
                stop = min((i + 1) * TILE, (k + 1) * band)
                for j in range(3):
                    piece = block(i, j, at - i * TILE, stop - i * TILE)
                    gram[at - k * band : stop - k * band, j * TILE : (j + 1) * TILE] = piece
                at = stop

    for s in range(2):
        cols = slice(s * width, (s + 1) * width)
        cross = lax.dot_general(
            left[...],
            full[:, cols],
            (((0,), (0,)), ((), ())),
            precision=lax.Precision.HIGHEST,
            preferred_element_type=jnp.float32,
        )
        extra = jnp.where(kind == s, gram[...] * (1.0 / norm), 0.0)
        normal_ref[:, cols] = cross * (1.0 / full.shape[0]) + extra


def call(kernel, outs, args, scratch=(), scalars=0):
    smem = [pl.BlockSpec(memory_space=pltpu.SMEM)] * scalars
    vmem = [pl.BlockSpec(memory_space=pltpu.VMEM)] * (len(args) - scalars)
    many = isinstance(outs, (list, tuple))
    out_specs = pl.BlockSpec(memory_space=pltpu.VMEM)
    return pl.pallas_call(
        kernel,
        out_shape=outs,
        in_specs=smem + vmem,
        out_specs=[out_specs] * len(outs) if many else out_specs,
        scratch_shapes=list(scratch),
        compiler_params=pltpu.CompilerParams(vmem_limit_bytes=VMEM_LIMIT),
    )(*args)


def exchange(values, axes):
    flat = values.reshape(-1, values.shape[-1])
    return lax.all_to_all(flat, axes, 0, 0, tiled=True).reshape(values.shape)


def shards(desc, species, atom_cfg, slot, weights):
    atoms, width = desc.shape
    configs = slot.shape[0]
    cfg_here = weights.shape[0]
    n_dev = math.prod(SIZES)
    core, kind, part = lax.axis_index("c"), lax.axis_index("h"), lax.axis_index("y")
    owner = (lax.axis_index("x") * 4 + lax.axis_index("l")) * 2 + core
    f32 = jnp.float32

    def shape(*dims):
        return jax.ShapeDtypeStruct(dims, f32)

    root = jnp.broadcast_to(jnp.sqrt(weights)[:, None], (cfg_here, 128))
    swap = [((l * 2 + h) * 4 + y, (y * 2 + h) * 4 + l) for l in range(4) for h in range(2) for y in range(4)]
    root_here = lax.ppermute(root, ("l", "h", "y"), swap)

    keep, send = call(
        local_kernel,
        [shape(16, 144, TILE), shape(16, 144, TILE)],
        [core[None], desc, species[None], atom_cfg[None], slot[None]],
        [pltpu.VMEM((width, atoms), jnp.bfloat16)],
        1,
    )
    flip = [(0, 1), (1, 0)]
    paired = call(add_kernel, shape(16, 144, TILE), [keep, lax.ppermute(send, "c", flip)])
    planes = call(plane_kernel, shape(8, 96, TILE), [exchange(paired, ("x", "y"))])
    scale = 1.0 / math.sqrt(atoms * n_dev / configs)
    spread = call(
        lambda *refs: spread_kernel(scale, *refs),
        shape(16, 96, TILE),
        [exchange(planes, ("l", "h")), root_here],
    )
    mine = exchange(spread, ("x", "y"))
    other = lax.ppermute(mine, "c", flip)
    band = 2 * width // 8
    norm = atoms * n_dev // 8
    normal, rows = call(
        lambda *refs: final_kernel(norm, *refs),
        [shape(band, 2 * width), shape(cfg_here, band)],
        [jnp.stack([core, kind, part, owner]), mine, other, root],
        [
            pltpu.VMEM((configs, 2 * width), f32),
            pltpu.VMEM((configs, band), f32),
            pltpu.VMEM((band, width), f32),
        ],
        1,
    )
    return normal, rows


def solution(mesh):
    fine = Mesh(mesh.devices.reshape(SIZES), AXES)
    return jax.shard_map(
        shards,
        mesh=fine,
        in_specs=(P(AXES, None), P(AXES), P(AXES), P(), P(("x", "l", "c"))),
        out_specs=(P(("h", "y"), None), P(("x", "l", "c"), ("h", "y"))),
        check_vma=False,
    )
```

```python
import math

import jax
import jax.numpy as jnp
from jax import lax
from jax.experimental import pallas as pl
from jax.experimental.pallas import tpu as pltpu
from jax.sharding import Mesh, PartitionSpec as P

AXES = ("x", "l", "c", "h", "y")
SIZES = (4, 4, 2, 2, 4)
TILE = 256
OFF = ((0, 1), (0, 2), (1, 2))
VMEM_LIMIT = 56 << 20


def split(core, first, second, keep_ref, send_ref, start, size):
    keep_ref[:, start : start + size, :] = jnp.where(core == 0, first, second)
    send_ref[:, start : start + size, :] = jnp.where(core == 0, second, first)


def sums_kernel(core_ref, desc_ref, species_ref, cfg_ref, slot_ref, keep_ref, send_ref):
    core = core_ref[0]
    atoms = desc_ref.shape[0]
    configs = slot_ref.shape[1]
    ids = lax.broadcasted_iota(jnp.int32, (configs, atoms), 0)
    member = (cfg_ref[...] == ids).astype(jnp.bfloat16)
    rows = lax.broadcasted_iota(jnp.int32, (configs, configs), 0)
    place = (slot_ref[...] == rows).astype(jnp.bfloat16)
    placed = jnp.dot(place, member, preferred_element_type=jnp.float32).astype(jnp.bfloat16)
    for kind in range(2):
        mask = (species_ref[...] == kind).astype(jnp.bfloat16)
        sums = jnp.dot(placed * mask, desc_ref[...], preferred_element_type=jnp.float32)
        for j in range(3):
            tile = sums[:, j * TILE : (j + 1) * TILE].reshape(16, 2, 8, TILE)
            split(core, tile[:, 0], tile[:, 1], keep_ref, send_ref, (kind * 3 + j) * 8, 8)


def gram_kernel(off_ref, desc_ref, species_ref, out_ref):
    def tiles(pairs):
        turned = {}
        for b, (i, j) in enumerate(pairs):
            if i not in turned:
                turned[i] = desc_ref[:, i * TILE : (i + 1) * TILE].T
            for kind in range(2):
                mask = (species_ref[...] == kind).astype(jnp.bfloat16)
                tile = jnp.dot(
                    turned[i] * mask, desc_ref[:, j * TILE : (j + 1) * TILE], preferred_element_type=jnp.float32
                )
                start = (kind * 3 + b) * 16
                out_ref[:, start : start + 16, :] = tile.reshape(16, 16, TILE)

    @pl.when(off_ref[0] == 1)
    def _():
        tiles(OFF)

    @pl.when(off_ref[0] == 0)
    def _():
        tiles(((0, 0), (1, 1), (2, 2)))


def final_kernel(
    norm, pos_ref, mine_ref, other_ref, root_ref, normal_ref, cfg_ref, full, left, gram
):
    core, kind, part, owner = pos_ref[0], pos_ref[1], pos_ref[2], pos_ref[3]
    width = gram.shape[1]
    band = left.shape[1]

    def half(which, start, size):
        a = mine_ref[:, start : start + size, :]
        b = other_ref[:, start : start + size, :]
        return jnp.where(core == which, a, b)

    for j in range(6):
        pair = [half(which, 48 + 8 * j, 8)[:, None] for which in range(2)]
        full[:, j * TILE : (j + 1) * TILE] = jnp.concatenate(pair, 1).reshape(256, TILE)

    def off(b):
        return half(0, 16 * b, 16).reshape(TILE, TILE)

    def diag(b):
        return half(1, 16 * b, 16).reshape(TILE, TILE)

    def block(i, j, lo, hi):
        if i == j:
            return diag(i)[lo:hi]
        if i < j:
            return off(OFF.index((i, j)))[lo:hi]
        return off(OFF.index((j, i)))[:, lo:hi].T

    for k in range(4):

        @pl.when(part == k)
        def _():
            cols = slice(k * band, (k + 1) * band)
            shifted = slice(width + k * band, width + (k + 1) * band)
            left[...] = jnp.where(kind == 0, full[:, cols], full[:, shifted])
            own = pl.ds(pl.multiple_of(owner * 8, 8), 8)
            tile = jnp.where(kind == 0, full[own, cols], full[own, shifted])
            cfg_ref[...] = tile / root_ref[:, :1]
            at = k * band
            while at < (k + 1) * band:
                i = at // TILE
                stop = min((i + 1) * TILE, (k + 1) * band)
                for j in range(3):
                    piece = block(i, j, at - i * TILE, stop - i * TILE)
                    gram[at - k * band : stop - k * band, j * TILE : (j + 1) * TILE] = piece
                at = stop

    for s in range(2):
        cols = slice(s * width, (s + 1) * width)
        cross = lax.dot_general(
            left[...],
            full[:, cols],
            (((0,), (0,)), ((), ())),
            precision=lax.Precision.HIGHEST,
            preferred_element_type=jnp.float32,
        )
        extra = jnp.where(kind == s, gram[...] * (1.0 / norm), 0.0)
        normal_ref[:, cols] = cross * (1.0 / full.shape[0]) + extra


def call(kernel, outs, args, scratch=(), scalars=0):
    smem = [pl.BlockSpec(memory_space=pltpu.SMEM)] * scalars
    vmem = [pl.BlockSpec(memory_space=pltpu.VMEM)] * (len(args) - scalars)
    many = isinstance(outs, (list, tuple))
    out_specs = pl.BlockSpec(memory_space=pltpu.VMEM)
    return pl.pallas_call(
        kernel,
        out_shape=outs,
        in_specs=smem + vmem,
        out_specs=[out_specs] * len(outs) if many else out_specs,
        scratch_shapes=list(scratch),
        compiler_params=pltpu.CompilerParams(vmem_limit_bytes=VMEM_LIMIT),
    )(*args)


def exchange(values, axes):
    flat = values.reshape(-1, values.shape[-1])
    return lax.all_to_all(flat, axes, 0, 0, tiled=True).reshape(values.shape)


def shards(desc, species, atom_cfg, slot, weights):
    atoms, width = desc.shape
    configs = slot.shape[0]
    cfg_here = weights.shape[0]
    n_dev = math.prod(SIZES)
    core, kind, part = lax.axis_index("c"), lax.axis_index("h"), lax.axis_index("y")
    owner = (lax.axis_index("x") * 4 + lax.axis_index("l")) * 2 + core
    f32 = jnp.float32

    def shape(*dims):
        return jax.ShapeDtypeStruct(dims, f32)

    root = jnp.broadcast_to(jnp.sqrt(weights)[:, None], (cfg_here, 128))
    swap = [((l * 2 + h) * 4 + y, (y * 2 + h) * 4 + l) for l in range(4) for h in range(2) for y in range(4)]
    root_here = lax.ppermute(root, ("l", "h", "y"), swap)

    flip = [(0, 1), (1, 0)]
    scale = 1.0 / math.sqrt(atoms * n_dev / configs)
    keep_s, send_s = call(
        sums_kernel,
        [shape(16, 48, TILE)] * 2,
        [core[None], desc, species[None], atom_cfg[None], slot[None]],
        scalars=1,
    )
    keep_s, send_s, desc = lax.optimization_barrier((keep_s, send_s, desc))
    send_g = call(gram_kernel, shape(16, 96, TILE), [core[None], desc, species[None]], scalars=1)
    came_s, root_here = lax.optimization_barrier((lax.ppermute(send_s, "c", flip), root_here))
    send_g, sums, desc = lax.optimization_barrier((send_g, keep_s + came_s, desc))
    keep_g = call(gram_kernel, shape(16, 96, TILE), [1 - core[None], desc, species[None]], scalars=1)
    grams = keep_g + lax.ppermute(send_g, "c", flip)
    sums = jnp.sum(exchange(sums, ("x", "y")), 0)
    grams = jnp.sum(exchange(grams, ("x", "y")), 0)
    planes = jnp.stack([jnp.concatenate([grams[:48], sums]), jnp.concatenate([grams[48:], sums])])
    planes = jnp.broadcast_to(planes[None], (4, 2, 96, TILE)).reshape(8, 96, TILE)
    total = jnp.sum(exchange(planes, ("l", "h")), 0)
    factor = jnp.concatenate([jnp.ones((48, 1), f32), jnp.tile(root_here[:, :1] * scale, (6, 1))])
    mine = exchange(jnp.broadcast_to(total * factor, (16, 96, TILE)), ("x", "y"))
    other = lax.ppermute(mine, "c", flip)
    band = 2 * width // 8
    norm = atoms * n_dev // 8
    normal, rows = call(
        lambda *refs: final_kernel(norm, *refs),
        [shape(band, 2 * width), shape(cfg_here, band)],
        [jnp.stack([core, kind, part, owner]), mine, other, root],
        [
            pltpu.VMEM((configs, 2 * width), f32),
            pltpu.VMEM((configs, band), f32),
            pltpu.VMEM((band, width), f32),
        ],
        1,
    )
    return normal, rows


def solution(mesh):
    fine = Mesh(mesh.devices.reshape(SIZES), AXES)
    return jax.shard_map(
        shards,
        mesh=fine,
        in_specs=(P(AXES, None), P(AXES), P(AXES), P(), P(("x", "l", "c"))),
        out_specs=(P(("h", "y"), None), P(("x", "l", "c"), ("h", "y"))),
        check_vma=False,
    )
```

```python
import math

import jax
import jax.numpy as jnp
from jax import lax
from jax.experimental import pallas as pl
from jax.experimental.pallas import tpu as pltpu
from jax.sharding import Mesh, PartitionSpec as P

AXES = ("x", "l", "c", "h", "y")
SIZES = (4, 4, 2, 2, 4)
TILE = 256
LANES = 128
PAIRS = ((0, 1), (0, 2), (1, 2), (0, 0), (1, 1), (2, 2))
VMEM_LIMIT = 40 << 20


def local_kernel(core_ref, desc_ref, species_ref, cfg_ref, slot_ref, keep_ref, send_ref):
    core = core_ref[0]
    atoms, width = desc_ref.shape
    configs = slot_ref.shape[1]

    def put(block, first):
        for half in range(block.shape[1] // LANES):
            tile = block[:, half * LANES : (half + 1) * LANES].reshape(16, 2, 8, LANES)
            at = slice((first + half) * 8, (first + half + 1) * 8)
            keep_ref[:, at, :] = jnp.where(core == 0, tile[:, 0], tile[:, 1])
            send_ref[:, at, :] = jnp.where(core == 0, tile[:, 1], tile[:, 0])

    ids = lax.broadcasted_iota(jnp.int32, (configs, atoms), 0)
    member = (cfg_ref[...] == ids).astype(jnp.bfloat16)
    rows = lax.broadcasted_iota(jnp.int32, (configs, configs), 0)
    place = (slot_ref[...] == rows).astype(jnp.bfloat16)
    placed = jnp.dot(place, member, preferred_element_type=jnp.float32).astype(jnp.bfloat16)
    masks = [(species_ref[...] == kind).astype(jnp.bfloat16) for kind in range(2)]
    for kind in range(2):
        put(jnp.dot(placed * masks[kind], desc_ref[...], preferred_element_type=jnp.float32), 24 + kind * 6)
    for i in range(3):
        turned = desc_ref[:, i * TILE : (i + 1) * TILE].T
        for kind in range(2):
            left = turned * masks[kind]
            for j in range(i, 3):
                right = desc_ref[:, j * TILE : (j + 1) * TILE]
                put(
                    jnp.dot(left, right, preferred_element_type=jnp.float32),
                    kind * 12 + PAIRS.index((i, j)) * 2,
                )


def final_kernel(norm, pos_ref, mine_ref, other_ref, root_ref, normal_ref, cfg_ref, full, left, gram):
    core, kind, part, owner = pos_ref[0], pos_ref[1], pos_ref[2], pos_ref[3]
    width = gram.shape[1]
    band = left.shape[1]

    def joined(tile, lo=0, hi=16):
        at = slice(tile * 8, (tile + 1) * 8)
        a, b = mine_ref[lo:hi, at, :], other_ref[lo:hi, at, :]
        pair = [jnp.where(core == which, a, b)[:, None] for which in range(2)]
        return jnp.concatenate(pair, 1).reshape((hi - lo) * 16, LANES)

    for j in range(2 * width // LANES):
        full[:, j * LANES : (j + 1) * LANES] = joined(6 + j)

    def fill(row, col, piece):
        gram[row : row + piece.shape[0], col : col + piece.shape[1]] = piece

    def straight(tiles, lo, hi, row, col):
        for k, tile in enumerate(tiles):
            fill(row, col + k * LANES, joined(tile, lo, hi))

    def band_0():
        straight((4, 5, 0, 1, 2, 3), 0, 12, 0, 0)

    def band_1():
        straight((2, 3, 0, 1, 4, 5), 12, 16, 0, 0)
        fill(64, 0, joined(0).T)
        straight((1, 2, 3, 4), 0, 8, 64, TILE)

    def band_2():
        fill(0, 0, joined(0).T)
        straight((4, 5, 2, 3), 8, 16, 0, TILE)
        fill(128, 0, joined(1).T[:64])
        fill(128, TILE, joined(2).T[:64])
        straight((3, 4), 0, 4, 128, 2 * TILE)

    def band_3():
        fill(0, 0, joined(0).T[64:])
        fill(64, 0, joined(1).T)
        fill(0, TILE, joined(2).T[64:])
        fill(64, TILE, joined(3).T)
        straight((4, 5), 4, 16, 0, 2 * TILE)

    for k, body in enumerate((band_0, band_1, band_2, band_3)):

        @pl.when(part == k)
        def _():
            cols = slice(k * band, (k + 1) * band)
            shifted = slice(width + k * band, width + (k + 1) * band)
            left[...] = jnp.where(kind == 0, full[:, cols], full[:, shifted])
            own = pl.ds(pl.multiple_of(owner * 8, 8), 8)
            tile = jnp.where(kind == 0, full[own, cols], full[own, shifted])
            cfg_ref[...] = tile / root_ref[:, :1]
            body()

    for s in range(2):
        cols = slice(s * width, (s + 1) * width)
        cross = lax.dot_general(
            left[...],
            full[:, cols],
            (((0,), (0,)), ((), ())),
            precision=lax.Precision.HIGHEST,
            preferred_element_type=jnp.float32,
        )
        extra = jnp.where(kind == s, gram[...] * (1.0 / norm), 0.0)
        normal_ref[:, cols] = cross * (1.0 / full.shape[0]) + extra


def call(kernel, outs, args, scratch=(), scalars=0):
    smem = [pl.BlockSpec(memory_space=pltpu.SMEM)] * scalars
    vmem = [pl.BlockSpec(memory_space=pltpu.VMEM)] * (len(args) - scalars)
    return pl.pallas_call(
        kernel,
        out_shape=outs,
        in_specs=smem + vmem,
        out_specs=[pl.BlockSpec(memory_space=pltpu.VMEM)] * len(outs),
        scratch_shapes=list(scratch),
        compiler_params=pltpu.CompilerParams(vmem_limit_bytes=VMEM_LIMIT),
    )(*args)


def exchange(values, axes):
    flat = values.reshape(-1, values.shape[-1])
    return lax.all_to_all(flat, axes, 0, 0, tiled=True).reshape(values.shape)


def needed(grams, owner):
    def pick(*tiles):
        return jnp.concatenate([grams[8 * k : 8 * k + 8] for k in tiles])

    band_1 = jnp.where(owner >= 12, pick(1, 6, 7, 2, 3), pick(8, 9, 4, 5, 5))
    band_2 = jnp.where(owner >= 8, pick(5, 8, 9), pick(10, 11, 11))
    return jnp.stack(
        [
            pick(0, 1, 2, 3, 6, 7),
            jnp.concatenate([pick(0), band_1]),
            jnp.concatenate([pick(1, 2, 4), band_2]),
            pick(2, 3, 4, 5, 10, 11),
        ]
    )


def shards(desc, species, atom_cfg, slot, weights):
    atoms, width = desc.shape
    configs = slot.shape[0]
    cfg_here = weights.shape[0]
    n_dev = math.prod(SIZES)
    x, l, core, kind, part = [lax.axis_index(axis) for axis in AXES]
    f32 = jnp.float32

    root = jnp.broadcast_to(jnp.sqrt(weights)[:, None], (cfg_here, LANES))
    swap = [((a * 2 + h) * 4 + b, (b * 2 + h) * 4 + a) for a in range(4) for h in range(2) for b in range(4)]
    root_here = lax.ppermute(root, ("l", "h", "y"), swap)
    pos = jnp.stack([core, kind, part, (x * 4 + l) * 2 + core])

    flip = [(0, 1), (1, 0)]
    payload = pltpu.VMEM((16, 288, LANES), f32)
    keep, send = call(
        local_kernel,
        [payload, payload],
        [core[None], desc, species[None], atom_cfg[None], slot[None]],
        scalars=1,
    )
    came, root_here, pos = lax.optimization_barrier((lax.ppermute(send, "c", flip), root_here, pos))
    total = jnp.sum(exchange(keep + came, ("x", "y")), 0)
    grams, sums = total[:192].reshape(2, 96, LANES), total[192:]
    planes = jnp.concatenate([grams, jnp.broadcast_to(sums[None], (2, 96, LANES))], 1)
    planes = jnp.broadcast_to(planes[None], (4, 2, 192, LANES)).reshape(8, 192, LANES)
    total = jnp.sum(exchange(planes, ("l", "h")), 0)
    scale = 1.0 / math.sqrt(atoms * n_dev / configs)
    sums = (total[96:].reshape(12, 8, LANES) * (root_here * scale)).reshape(96, LANES)
    bands = needed(total[:96], x * 4 + part)
    spread = jnp.concatenate([bands, jnp.broadcast_to(sums[None], (4, 96, LANES))], 1)
    spread = jnp.broadcast_to(spread[None], (4, 4, 144, LANES)).reshape(16, 144, LANES)
    mine = exchange(spread, ("x", "y"))
    other = lax.ppermute(mine, "c", flip)
    band = 2 * width // 8
    norm = atoms * n_dev // 8
    normal, rows = call(
        lambda *refs: final_kernel(norm, *refs),
        [jax.ShapeDtypeStruct((band, 2 * width), f32), jax.ShapeDtypeStruct((cfg_here, band), f32)],
        [pos] + [pltpu.with_memory_space_constraint(a, pltpu.VMEM) for a in (mine, other)] + [root],
        [
            pltpu.VMEM((configs, 2 * width), f32),
            pltpu.VMEM((configs, band), f32),
            pltpu.VMEM((band, width), f32),
        ],
        1,
    )
    return normal, rows


def solution(mesh):
    fine = Mesh(mesh.devices.reshape(SIZES), AXES)
    return jax.shard_map(
        shards,
        mesh=fine,
        in_specs=(P(AXES, None), P(AXES), P(AXES), P(), P(("x", "l", "c"))),
        out_specs=(P(("h", "y"), None), P(("x", "l", "c"), ("h", "y"))),
        check_vma=False,
    )
```

```python
import math

import jax
import jax.numpy as jnp
from jax import lax
from jax.experimental import pallas as pl
from jax.experimental.pallas import tpu as pltpu
from jax.sharding import Mesh, PartitionSpec as P

AXES = ("x", "l", "c", "h", "y")
SIZES = (4, 4, 2, 2, 4)
TILE = 256
LANES = 128
PAIRS = ((0, 1), (0, 2), (1, 2), (0, 0), (1, 1), (2, 2))


def local_kernel(
    core_ref,
    desc_hbm,
    species_hbm,
    cfg_hbm,
    slot_hbm,
    keep_ref,
    send_ref,
    desc_ref,
    species_ref,
    cfg_ref,
    slot_ref,
    turned,
    sems,
):
    core = core_ref[0]
    atoms, width = desc_ref.shape
    configs = slot_ref.shape[1]
    small = ((cfg_hbm, cfg_ref), (slot_hbm, slot_ref), (species_hbm, species_ref))
    copies = [pltpu.make_async_copy(a, b, sems.at[k]) for k, (a, b) in enumerate(small)]
    for i in range(3):
        cols = slice(i * TILE, (i + 1) * TILE)
        copies.append(pltpu.make_async_copy(desc_hbm.at[:, cols], desc_ref.at[:, cols], sems.at[3 + i]))
    for copy in copies:
        copy.start()
    for copy in copies[:3]:
        copy.wait()

    def put(block, first):
        for half in range(block.shape[1] // LANES):
            tile = block[:, half * LANES : (half + 1) * LANES].reshape(16, 2, 8, LANES)
            at = slice((first + half) * 8, (first + half + 1) * 8)
            keep_ref[:, at, :] = jnp.where(core == 0, tile[:, 0], tile[:, 1])
            send_ref[:, at, :] = jnp.where(core == 0, tile[:, 1], tile[:, 0])

    ids = lax.broadcasted_iota(jnp.int32, (configs, atoms), 0)
    member = (cfg_ref[...] == ids).astype(jnp.bfloat16)
    rows = lax.broadcasted_iota(jnp.int32, (configs, configs), 0)
    place = (slot_ref[...] == rows).astype(jnp.bfloat16)
    placed = jnp.dot(place, member, preferred_element_type=jnp.float32).astype(jnp.bfloat16)
    masks = [(species_ref[...] == kind).astype(jnp.bfloat16) for kind in range(2)]
    members = [placed * mask for mask in masks]
    for j in range(3):
        copies[3 + j].wait()
        right = desc_ref[:, j * TILE : (j + 1) * TILE]
        for kind in range(2):
            put(jnp.dot(members[kind], right, preferred_element_type=jnp.float32), 24 + kind * 6 + j * 2)
        turned[j * TILE : (j + 1) * TILE, :] = right.T
        for i in range(j + 1):
            for kind in range(2):
                left = turned[i * TILE : (i + 1) * TILE, :] * masks[kind]
                block = jnp.dot(left, right, preferred_element_type=jnp.float32)
                put(block, kind * 12 + PAIRS.index((i, j)) * 2)


def final_kernel(norm, pos_ref, mine_ref, other_ref, root_ref, normal_ref, cfg_ref, full, left, gram):
    core, kind, part, owner = pos_ref[0], pos_ref[1], pos_ref[2], pos_ref[3]
    width = gram.shape[1]
    band = left.shape[1]

    def joined(tile, lo=0, hi=16):
        at = slice(tile * 8, (tile + 1) * 8)
        a, b = mine_ref[lo:hi, at, :], other_ref[lo:hi, at, :]
        pair = [jnp.where(core == which, a, b)[:, None] for which in range(2)]
        return jnp.concatenate(pair, 1).reshape((hi - lo) * 16, LANES)

    for j in range(2 * width // LANES):
        full[:, j * LANES : (j + 1) * LANES] = joined(6 + j)

    def fill(row, col, piece):
        gram[row : row + piece.shape[0], col : col + piece.shape[1]] = piece

    def straight(tiles, lo, hi, row, col):
        for k, tile in enumerate(tiles):
            fill(row, col + k * LANES, joined(tile, lo, hi))

    def band_0():
        straight((4, 5, 0, 1, 2, 3), 0, 12, 0, 0)

    def band_1():
        straight((2, 3, 0, 1, 4, 5), 12, 16, 0, 0)
        fill(64, 0, joined(0).T)
        straight((1, 2, 3, 4), 0, 8, 64, TILE)

    def band_2():
        fill(0, 0, joined(0).T)
        straight((4, 5, 2, 3), 8, 16, 0, TILE)
        fill(128, 0, joined(1).T[:64])
        fill(128, TILE, joined(2).T[:64])
        straight((3, 4), 0, 4, 128, 2 * TILE)

    def band_3():
        fill(0, 0, joined(0).T[64:])
        fill(64, 0, joined(1).T)
        fill(0, TILE, joined(2).T[64:])
        fill(64, TILE, joined(3).T)
        straight((4, 5), 4, 16, 0, 2 * TILE)

    for k, body in enumerate((band_0, band_1, band_2, band_3)):

        @pl.when(part == k)
        def _():
            cols = slice(k * band, (k + 1) * band)
            shifted = slice(width + k * band, width + (k + 1) * band)
            left[...] = jnp.where(kind == 0, full[:, cols], full[:, shifted])
            own = pl.ds(pl.multiple_of(owner * 8, 8), 8)
            tile = jnp.where(kind == 0, full[own, cols], full[own, shifted])
            cfg_ref[...] = tile / root_ref[:, :1]
            body()

    for s in range(2):
        cols = slice(s * width, (s + 1) * width)
        cross = lax.dot_general(
            left[...],
            full[:, cols],
            (((0,), (0,)), ((), ())),
            precision=lax.Precision.HIGHEST,
            preferred_element_type=jnp.float32,
        )
        extra = jnp.where(kind == s, gram[...] * (1.0 / norm), 0.0)
        normal_ref[:, cols] = cross * (1.0 / full.shape[0]) + extra


def call(kernel, outs, args, scratch, space, limit):
    smem = pl.BlockSpec(memory_space=pltpu.SMEM)
    held = [pltpu.with_memory_space_constraint(a, space) for a in args[1:]]
    return pl.pallas_call(
        kernel,
        out_shape=outs,
        in_specs=[smem] + [pl.BlockSpec(memory_space=space)] * len(held),
        out_specs=[pl.BlockSpec(memory_space=pltpu.VMEM)] * len(outs),
        scratch_shapes=list(scratch),
        compiler_params=pltpu.CompilerParams(vmem_limit_bytes=limit),
    )(args[0], *held)


def exchange(values, axes):
    flat = values.reshape(-1, values.shape[-1])
    return lax.all_to_all(flat, axes, 0, 0, tiled=True).reshape(values.shape)


def needed(grams, owner):
    def pick(*tiles):
        return jnp.concatenate([grams[8 * k : 8 * k + 8] for k in tiles])

    band_1 = jnp.where(owner >= 12, pick(1, 6, 7, 2, 3), pick(8, 9, 4, 5, 5))
    band_2 = jnp.where(owner >= 8, pick(5, 8, 9), pick(10, 11, 11))
    return jnp.stack(
        [
            pick(0, 1, 2, 3, 6, 7),
            jnp.concatenate([pick(0), band_1]),
            jnp.concatenate([pick(1, 2, 4), band_2]),
            pick(2, 3, 4, 5, 10, 11),
        ]
    )


def shards(desc, species, atom_cfg, slot, weights):
    atoms, width = desc.shape
    configs = slot.shape[0]
    cfg_here = weights.shape[0]
    n_dev = math.prod(SIZES)
    x, l, core, kind, part = [lax.axis_index(axis) for axis in AXES]
    f32 = jnp.float32

    root = jnp.broadcast_to(jnp.sqrt(weights)[:, None], (cfg_here, LANES))
    pos = jnp.stack([core, kind, part, (x * 4 + l) * 2 + core])

    flip = [(0, 1), (1, 0)]
    payload = pltpu.VMEM((16, 288, LANES), f32)
    int_row = pltpu.VMEM((1, atoms), jnp.int32)
    keep, send = call(
        local_kernel,
        [payload, payload],
        [core[None], desc, species[None], atom_cfg[None], slot[None]],
        [
            pltpu.VMEM((atoms, width), jnp.bfloat16),
            int_row,
            int_row,
            pltpu.VMEM((1, configs), jnp.int32),
            pltpu.VMEM((width, atoms), jnp.bfloat16),
            pltpu.SemaphoreType.DMA((6,)),
        ],
        pltpu.HBM,
        24 << 20,
    )
    came, root, pos = lax.optimization_barrier((lax.ppermute(send, "c", flip), root, pos))
    total = jnp.sum(exchange(keep + came, ("x", "y")), 0)
    grams, sums = total[:192].reshape(2, 96, LANES), total[192:]
    planes = jnp.concatenate([grams, jnp.broadcast_to(jnp.concatenate([sums, root])[None], (2, 104, LANES))], 1)
    planes = jnp.broadcast_to(planes[None], (4, 2, 200, LANES)).reshape(8, 200, LANES)
    got = exchange(planes, ("l", "h"))
    root_here = lax.dynamic_index_in_dim(got, part * 2, 0, False)[192:]
    total = jnp.sum(got[:, :192], 0)
    scale = 1.0 / math.sqrt(atoms * n_dev / configs)
    sums = (total[96:].reshape(12, 8, LANES) * (root_here * scale)).reshape(96, LANES)
    bands = needed(total[:96], x * 4 + part)
    spread = jnp.concatenate([bands, jnp.broadcast_to(sums[None], (4, 96, LANES))], 1)
    spread = jnp.broadcast_to(spread[None], (4, 4, 144, LANES)).reshape(16, 144, LANES)
    mine = exchange(spread, ("x", "y"))
    other = lax.ppermute(mine, "c", flip)
    band = 2 * width // 8
    norm = atoms * n_dev // 8
    normal, rows = call(
        lambda *refs: final_kernel(norm, *refs),
        [jax.ShapeDtypeStruct((band, 2 * width), f32), jax.ShapeDtypeStruct((cfg_here, band), f32)],
        [pos, mine, other, root],
        [
            pltpu.VMEM((configs, 2 * width), f32),
            pltpu.VMEM((configs, band), f32),
            pltpu.VMEM((band, width), f32),
        ],
        pltpu.VMEM,
        24 << 20,
    )
    return normal, rows


def solution(mesh):
    fine = Mesh(mesh.devices.reshape(SIZES), AXES)
    return jax.shard_map(
        shards,
        mesh=fine,
        in_specs=(P(AXES, None), P(AXES), P(AXES), P(), P(("x", "l", "c"))),
        out_specs=(P(("h", "y"), None), P(("x", "l", "c"), ("h", "y"))),
        check_vma=False,
    )
```

```python
import math

import jax
import jax.numpy as jnp
from jax import lax
from jax.experimental import pallas as pl
from jax.experimental.pallas import tpu as pltpu
from jax.sharding import Mesh, PartitionSpec as P

AXES = ("x", "l", "c", "h", "y")
SIZES = (4, 4, 2, 2, 4)
TILE = 256
LANES = 128
PAIRS = ((0, 1), (0, 2), (1, 2), (0, 0), (1, 1), (2, 2))


def put(core, block, first, keep_ref, send_ref):
    for half in range(block.shape[1] // LANES):
        tile = block[:, half * LANES : (half + 1) * LANES].reshape(16, 2, 8, LANES)
        at = slice((first + half) * 8, (first + half + 1) * 8)
        keep_ref[:, at, :] = jnp.where(core == 0, tile[:, 0], tile[:, 1])
        send_ref[:, at, :] = jnp.where(core == 0, tile[:, 1], tile[:, 0])


def load(small, desc_hbm, desc_ref, sems):
    copies = [pltpu.make_async_copy(a, b, sems.at[k]) for k, (a, b) in enumerate(small)]
    for i in range(3):
        cols = slice(i * TILE, (i + 1) * TILE)
        copies.append(pltpu.make_async_copy(desc_hbm.at[:, cols], desc_ref.at[:, cols], sems.at[3 + i]))
    for copy in copies:
        copy.start()
    for copy in copies[:-3]:
        copy.wait()
    return copies[-3:]


def sums_kernel(
    core_ref,
    desc_hbm,
    species_hbm,
    cfg_hbm,
    slot_hbm,
    keep_ref,
    send_ref,
    desc_ref,
    species_ref,
    cfg_ref,
    slot_ref,
    sems,
):
    core = core_ref[0]
    atoms = desc_ref.shape[0]
    configs = slot_ref.shape[1]
    small = ((cfg_hbm, cfg_ref), (slot_hbm, slot_ref), (species_hbm, species_ref))
    blocks = load(small, desc_hbm, desc_ref, sems)
    ids = lax.broadcasted_iota(jnp.int32, (configs, atoms), 0)
    member = (cfg_ref[...] == ids).astype(jnp.bfloat16)
    rows = lax.broadcasted_iota(jnp.int32, (configs, configs), 0)
    place = (slot_ref[...] == rows).astype(jnp.bfloat16)
    placed = jnp.dot(place, member, preferred_element_type=jnp.float32).astype(jnp.bfloat16)
    members = [placed * (species_ref[...] == kind).astype(jnp.bfloat16) for kind in range(2)]
    for j in range(3):
        blocks[j].wait()
        right = desc_ref[:, j * TILE : (j + 1) * TILE]
        for kind in range(2):
            block = jnp.dot(members[kind], right, preferred_element_type=jnp.float32)
            put(core, block, kind * 6 + j * 2, keep_ref, send_ref)


def gram_kernel(core_ref, desc_hbm, species_hbm, keep_ref, send_ref, desc_ref, species_ref, turned, sems):
    core = core_ref[0]
    blocks = load(((species_hbm, species_ref),), desc_hbm, desc_ref, sems)
    masks = [(species_ref[...] == kind).astype(jnp.bfloat16) for kind in range(2)]
    for j in range(3):
        blocks[j].wait()
        right = desc_ref[:, j * TILE : (j + 1) * TILE]
        turned[j * TILE : (j + 1) * TILE, :] = right.T
        for i in range(j + 1):
            for kind in range(2):
                left = turned[i * TILE : (i + 1) * TILE, :] * masks[kind]
                block = jnp.dot(left, right, preferred_element_type=jnp.float32)
                put(core, block, kind * 12 + PAIRS.index((i, j)) * 2, keep_ref, send_ref)


def final_kernel(
    norm, pos_ref, sums_ref, other_sums, gram_ref, other_gram, root_ref, normal_ref, cfg_ref, full, left, gram
):
    core, kind, part, owner = pos_ref[0], pos_ref[1], pos_ref[2], pos_ref[3]
    width = gram.shape[1]
    band = left.shape[1]

    def joined(tile, lo=0, hi=16, refs=(gram_ref, other_gram)):
        at = slice(tile * 8, (tile + 1) * 8)
        a, b = [ref[lo:hi, at, :] for ref in refs]
        pair = [jnp.where(core == which, a, b)[:, None] for which in range(2)]
        return jnp.concatenate(pair, 1).reshape((hi - lo) * 16, LANES)

    for j in range(2 * width // LANES):
        full[:, j * LANES : (j + 1) * LANES] = joined(j, refs=(sums_ref, other_sums))

    def fill(row, col, piece):
        gram[row : row + piece.shape[0], col : col + piece.shape[1]] = piece

    def straight(tiles, lo, hi, row, col):
        for k, tile in enumerate(tiles):
            fill(row, col + k * LANES, joined(tile, lo, hi))

    def band_0():
        straight((4, 5, 0, 1, 2, 3), 0, 12, 0, 0)

    def band_1():
        straight((2, 3, 0, 1, 4, 5), 12, 16, 0, 0)
        fill(64, 0, joined(0).T)
        straight((1, 2, 3, 4), 0, 8, 64, TILE)

    def band_2():
        fill(0, 0, joined(0).T)
        straight((4, 5, 2, 3), 8, 16, 0, TILE)
        fill(128, 0, joined(1).T[:64])
        fill(128, TILE, joined(2).T[:64])
        straight((3, 4), 0, 4, 128, 2 * TILE)

    def band_3():
        fill(0, 0, joined(0).T[64:])
        fill(64, 0, joined(1).T)
        fill(0, TILE, joined(2).T[64:])
        fill(64, TILE, joined(3).T)
        straight((4, 5), 4, 16, 0, 2 * TILE)

    for k, body in enumerate((band_0, band_1, band_2, band_3)):

        @pl.when(part == k)
        def _():
            cols = slice(k * band, (k + 1) * band)
            shifted = slice(width + k * band, width + (k + 1) * band)
            left[...] = jnp.where(kind == 0, full[:, cols], full[:, shifted])
            own = pl.ds(pl.multiple_of(owner * 8, 8), 8)
            tile = jnp.where(kind == 0, full[own, cols], full[own, shifted])
            cfg_ref[...] = tile / root_ref[:, :1]
            body()

    for s in range(2):
        cols = slice(s * width, (s + 1) * width)
        cross = lax.dot_general(
            left[...],
            full[:, cols],
            (((0,), (0,)), ((), ())),
            precision=lax.Precision.HIGHEST,
            preferred_element_type=jnp.float32,
        )
        extra = jnp.where(kind == s, gram[...] * (1.0 / norm), 0.0)
        normal_ref[:, cols] = cross * (1.0 / full.shape[0]) + extra


def call(kernel, outs, args, scratch, space, limit):
    smem = pl.BlockSpec(memory_space=pltpu.SMEM)
    held = [pltpu.with_memory_space_constraint(a, space) for a in args[1:]]
    return pl.pallas_call(
        kernel,
        out_shape=outs,
        in_specs=[smem] + [pl.BlockSpec(memory_space=space)] * len(held),
        out_specs=[pl.BlockSpec(memory_space=pltpu.VMEM)] * len(outs),
        scratch_shapes=list(scratch),
        compiler_params=pltpu.CompilerParams(vmem_limit_bytes=limit),
    )(args[0], *held)


def exchange(values, axes):
    flat = values.reshape(-1, values.shape[-1])
    return lax.all_to_all(flat, axes, 0, 0, tiled=True).reshape(values.shape)


def needed(grams, owner):
    def pick(*tiles):
        return jnp.concatenate([grams[8 * k : 8 * k + 8] for k in tiles])

    band_1 = jnp.where(owner >= 12, pick(1, 6, 7, 2, 3), pick(8, 9, 4, 5, 5))
    band_2 = jnp.where(owner >= 8, pick(5, 8, 9), pick(10, 11, 11))
    return jnp.stack(
        [
            pick(0, 1, 2, 3, 6, 7),
            jnp.concatenate([pick(0), band_1]),
            jnp.concatenate([pick(1, 2, 4), band_2]),
            pick(2, 3, 4, 5, 10, 11),
        ]
    )


def shards(desc, species, atom_cfg, slot, weights):
    atoms, width = desc.shape
    configs = slot.shape[0]
    cfg_here = weights.shape[0]
    n_dev = math.prod(SIZES)
    x, l, core, kind, part = [lax.axis_index(axis) for axis in AXES]
    f32 = jnp.float32

    root = jnp.broadcast_to(jnp.sqrt(weights)[:, None], (cfg_here, LANES))
    pos = jnp.stack([core, kind, part, (x * 4 + l) * 2 + core])

    flip = [(0, 1), (1, 0)]
    int_row = pltpu.VMEM((1, atoms), jnp.int32)
    matrix = pltpu.VMEM((atoms, width), jnp.bfloat16)
    sems = pltpu.SemaphoreType.DMA((6,))

    def tiles(count):
        return pltpu.VMEM((16, count * 8, LANES), f32)

    keep_s, send_s = call(
        sums_kernel,
        [tiles(12)] * 2,
        [core[None], desc, species[None], atom_cfg[None], slot[None]],
        [matrix, int_row, int_row, pltpu.VMEM((1, configs), jnp.int32), sems],
        pltpu.HBM,
        24 << 20,
    )
    pair_s, desc, pos, root = lax.optimization_barrier((keep_s + lax.ppermute(send_s, "c", flip), desc, pos, root))
    keep_g, send_g = call(
        gram_kernel,
        [tiles(24)] * 2,
        [core[None], desc, species[None]],
        [matrix, int_row, pltpu.VMEM((width, atoms), jnp.bfloat16), sems],
        pltpu.HBM,
        24 << 20,
    )
    pair_g = keep_g + lax.ppermute(send_g, "c", flip)
    plane_s = jnp.sum(exchange(pair_s, ("x", "y")), 0)
    plane_g = jnp.sum(exchange(pair_g, ("x", "y")), 0).reshape(2, 96, LANES)

    place = kind * 4 + l

    def along_z(value, k):
        pairs = [((z % 4) * 2 + z // 4, ((z + k) % 8 % 4) * 2 + (z + k) % 8 // 4) for z in range(8)]
        return lax.ppermute(value, ("l", "h"), pairs)

    far = (4, 3, 5, 2, 6, 1, 7)
    rooted = jnp.concatenate([plane_s, root])
    got = [(rooted, place)] + [(along_z(rooted, k), (place - k) % 8) for k in far]
    root_here = sum(jnp.where(source == part, value[96:], 0.0) for value, source in got)
    scale = 1.0 / math.sqrt(atoms * n_dev / configs)
    sums = sum(value[:96] for value, _ in got).reshape(12, 8, LANES) * (root_here * scale)
    mine_s = exchange(jnp.broadcast_to(sums.reshape(1, 96, LANES), (16, 96, LANES)), ("x", "y"))

    grams = lax.dynamic_index_in_dim(plane_g, kind, 0, False)
    for k in far:
        theirs = lax.dynamic_index_in_dim(plane_g, (place + k) % 8 // 4, 0, False)
        grams = grams + along_z(theirs, k)
    bands = needed(grams, x * 4 + part)
    mine_g = exchange(jnp.broadcast_to(bands[None], (4, 4, 48, LANES)).reshape(16, 48, LANES), ("x", "y"))
    band = 2 * width // 8
    norm = atoms * n_dev // 8
    normal, rows = call(
        lambda *refs: final_kernel(norm, *refs),
        [jax.ShapeDtypeStruct((band, 2 * width), f32), jax.ShapeDtypeStruct((cfg_here, band), f32)],
        [pos, mine_s, lax.ppermute(mine_s, "c", flip), mine_g, lax.ppermute(mine_g, "c", flip), root],
        [
            pltpu.VMEM((configs, 2 * width), f32),
            pltpu.VMEM((configs, band), f32),
            pltpu.VMEM((band, width), f32),
        ],
        pltpu.VMEM,
        24 << 20,
    )
    return normal, rows


def solution(mesh):
    fine = Mesh(mesh.devices.reshape(SIZES), AXES)
    return jax.shard_map(
        shards,
        mesh=fine,
        in_specs=(P(AXES, None), P(AXES), P(AXES), P(), P(("x", "l", "c"))),
        out_specs=(P(("h", "y"), None), P(("x", "l", "c"), ("h", "y"))),
        check_vma=False,
    )
```

```python
import math

import jax
import jax.numpy as jnp
from jax import lax
from jax.experimental import pallas as pl
from jax.experimental.pallas import tpu as pltpu
from jax.sharding import Mesh, PartitionSpec as P

AXES = ("x", "l", "c", "h", "y")
SIZES = (4, 4, 2, 2, 4)
TILE = 256
LANES = 128
PAIRS = ((0, 1), (0, 2), (1, 2), (0, 0), (1, 1), (2, 2))


def put(core, block, first, keep_ref, send_refs):
    for half in range(block.shape[1] // LANES):
        tile = block[:, half * LANES : (half + 1) * LANES].reshape(16, 2, 8, LANES)
        which, at = divmod((first + half) * 8, send_refs[0].shape[1])
        keep_ref[:, (first + half) * 8 : (first + half + 1) * 8, :] = jnp.where(core == 0, tile[:, 0], tile[:, 1])
        send_refs[which][:, at : at + 8, :] = jnp.where(core == 0, tile[:, 1], tile[:, 0])


def load(small, desc_hbm, desc_ref, sems):
    copies = [pltpu.make_async_copy(a, b, sems.at[k]) for k, (a, b) in enumerate(small)]
    for i in range(3):
        cols = slice(i * TILE, (i + 1) * TILE)
        copies.append(pltpu.make_async_copy(desc_hbm.at[:, cols], desc_ref.at[:, cols], sems.at[3 + i]))
    for copy in copies:
        copy.start()
    for copy in copies[:-3]:
        copy.wait()
    return copies[-3:]


def sums_kernel(
    core_ref,
    desc_hbm,
    species_hbm,
    cfg_hbm,
    slot_hbm,
    keep_ref,
    send_ref,
    desc_ref,
    species_ref,
    cfg_ref,
    slot_ref,
    sems,
):
    core = core_ref[0]
    atoms = desc_ref.shape[0]
    configs = slot_ref.shape[1]
    small = ((cfg_hbm, cfg_ref), (slot_hbm, slot_ref), (species_hbm, species_ref))
    blocks = load(small, desc_hbm, desc_ref, sems)
    ids = lax.broadcasted_iota(jnp.int32, (configs, atoms), 0)
    member = (cfg_ref[...] == ids).astype(jnp.bfloat16)
    rows = lax.broadcasted_iota(jnp.int32, (configs, configs), 0)
    place = (slot_ref[...] == rows).astype(jnp.bfloat16)
    placed = jnp.dot(place, member, preferred_element_type=jnp.float32).astype(jnp.bfloat16)
    members = [placed * (species_ref[...] == kind).astype(jnp.bfloat16) for kind in range(2)]
    for j in range(3):
        blocks[j].wait()
        right = desc_ref[:, j * TILE : (j + 1) * TILE]
        for kind in range(2):
            block = jnp.dot(members[kind], right, preferred_element_type=jnp.float32)
            put(core, block, kind * 6 + j * 2, keep_ref, [send_ref])


def gram_kernel(core_ref, desc_hbm, species_hbm, keep_ref, *refs):
    send_refs, (desc_ref, species_ref, turned, sems) = refs[:-4], refs[-4:]
    core = core_ref[0]
    blocks = load(((species_hbm, species_ref),), desc_hbm, desc_ref, sems)
    masks = [(species_ref[...] == kind).astype(jnp.bfloat16) for kind in range(2)]
    for j in range(3):
        blocks[j].wait()
        right = desc_ref[:, j * TILE : (j + 1) * TILE]
        turned[j * TILE : (j + 1) * TILE, :] = right.T
        for i in range(j + 1):
            for kind in range(2):
                left = turned[i * TILE : (i + 1) * TILE, :] * masks[kind]
                block = jnp.dot(left, right, preferred_element_type=jnp.float32)
                put(core, block, kind * 12 + PAIRS.index((i, j)) * 2, keep_ref, send_refs)


def final_kernel(norm, pos_ref, mine_ref, other_ref, root_ref, normal_ref, cfg_ref, full, left, gram):
    core, kind, part, owner = pos_ref[0], pos_ref[1], pos_ref[2], pos_ref[3]
    width = gram.shape[1]
    band = left.shape[1]

    def joined(tile, lo=0, hi=16):
        at = slice(tile * 8, (tile + 1) * 8)
        a, b = mine_ref[lo:hi, at, :], other_ref[lo:hi, at, :]
        pair = [jnp.where(core == which, a, b)[:, None] for which in range(2)]
        return jnp.concatenate(pair, 1).reshape((hi - lo) * 16, LANES)

    for j in range(2 * width // LANES):
        full[:, j * LANES : (j + 1) * LANES] = joined(6 + j)

    def fill(row, col, piece):
        gram[row : row + piece.shape[0], col : col + piece.shape[1]] = piece

    def straight(tiles, lo, hi, row, col):
        for k, tile in enumerate(tiles):
            fill(row, col + k * LANES, joined(tile, lo, hi))

    def band_0():
        straight((4, 5, 0, 1, 2, 3), 0, 12, 0, 0)

    def band_1():
        straight((2, 3, 0, 1, 4, 5), 12, 16, 0, 0)
        fill(64, 0, joined(0).T)
        straight((1, 2, 3, 4), 0, 8, 64, TILE)

    def band_2():
        fill(0, 0, joined(0).T)
        straight((4, 5, 2, 3), 8, 16, 0, TILE)
        fill(128, 0, joined(1).T[:64])
        fill(128, TILE, joined(2).T[:64])
        straight((3, 4), 0, 4, 128, 2 * TILE)

    def band_3():
        fill(0, 0, joined(0).T[64:])
        fill(64, 0, joined(1).T)
        fill(0, TILE, joined(2).T[64:])
        fill(64, TILE, joined(3).T)
        straight((4, 5), 4, 16, 0, 2 * TILE)

    for k, body in enumerate((band_0, band_1, band_2, band_3)):

        @pl.when(part == k)
        def _():
            cols = slice(k * band, (k + 1) * band)
            shifted = slice(width + k * band, width + (k + 1) * band)
            left[...] = jnp.where(kind == 0, full[:, cols], full[:, shifted])
            own = pl.ds(pl.multiple_of(owner * 8, 8), 8)
            tile = jnp.where(kind == 0, full[own, cols], full[own, shifted])
            cfg_ref[...] = tile / root_ref[:, :1]
            body()

    for s in range(2):
        cols = slice(s * width, (s + 1) * width)
        cross = lax.dot_general(
            left[...],
            full[:, cols],
            (((0,), (0,)), ((), ())),
            precision=lax.Precision.HIGHEST,
            preferred_element_type=jnp.float32,
        )
        extra = jnp.where(kind == s, gram[...] * (1.0 / norm), 0.0)
        normal_ref[:, cols] = cross * (1.0 / full.shape[0]) + extra


def call(kernel, outs, args, scratch, space, limit, flops):
    smem = pl.BlockSpec(memory_space=pltpu.SMEM)
    held = [pltpu.with_memory_space_constraint(a, space) for a in args[1:]]
    return pl.pallas_call(
        kernel,
        out_shape=outs,
        in_specs=[smem] + [pl.BlockSpec(memory_space=space)] * len(held),
        out_specs=[pl.BlockSpec(memory_space=pltpu.VMEM)] * len(outs),
        scratch_shapes=list(scratch),
        compiler_params=pltpu.CompilerParams(vmem_limit_bytes=limit),
        cost_estimate=pl.CostEstimate(flops=flops, bytes_accessed=8 << 20, transcendentals=0),
    )(args[0], *held)


def exchange(values, axes):
    flat = values.reshape(-1, values.shape[-1])
    return lax.all_to_all(flat, axes, 0, 0, tiled=True).reshape(values.shape)


def needed(grams, owner):
    def pick(*tiles):
        return jnp.concatenate([grams[8 * k : 8 * k + 8] for k in tiles])

    band_1 = jnp.where(owner >= 12, pick(1, 6, 7, 2, 3), pick(8, 9, 4, 5, 5))
    band_2 = jnp.where(owner >= 8, pick(5, 8, 9), pick(10, 11, 11))
    return jnp.stack(
        [
            pick(0, 1, 2, 3, 6, 7),
            jnp.concatenate([pick(0), band_1]),
            jnp.concatenate([pick(1, 2, 4), band_2]),
            pick(2, 3, 4, 5, 10, 11),
        ]
    )


def shards(desc, species, atom_cfg, slot, weights):
    atoms, width = desc.shape
    configs = slot.shape[0]
    cfg_here = weights.shape[0]
    n_dev = math.prod(SIZES)
    x, l, core, kind, part = [lax.axis_index(axis) for axis in AXES]
    f32 = jnp.float32

    root = jnp.broadcast_to(jnp.sqrt(weights)[:, None], (cfg_here, LANES))
    pos = jnp.stack([core, kind, part, (x * 4 + l) * 2 + core])

    flip = [(0, 1), (1, 0)]
    int_row = pltpu.VMEM((1, atoms), jnp.int32)
    matrix = pltpu.VMEM((atoms, width), jnp.bfloat16)
    sems = pltpu.SemaphoreType.DMA((6,))

    def tiles(count):
        return pltpu.VMEM((16, count * 8, LANES), f32)

    keep_s, send_s = call(
        sums_kernel,
        [tiles(12)] * 2,
        [core[None], desc, species[None], atom_cfg[None], slot[None]],
        [matrix, int_row, int_row, pltpu.VMEM((1, configs), jnp.int32), sems],
        pltpu.HBM,
        24 << 20,
        4 * configs * atoms * width,
    )
    pair_s, desc, pos, root = lax.optimization_barrier((keep_s + lax.ppermute(send_s, "c", flip), desc, pos, root))
    keep_g, *send_g = call(
        gram_kernel,
        [tiles(24)] + [tiles(6)] * 4,
        [core[None], desc, species[None]],
        [matrix, int_row, pltpu.VMEM((width, atoms), jnp.bfloat16), sems],
        pltpu.HBM,
        24 << 20,
        4 * width * width * atoms,
    )
    pair_g = keep_g + jnp.concatenate([lax.ppermute(part_g, "c", flip) for part_g in send_g], 1)
    plane_s = jnp.sum(exchange(pair_s, ("x", "y")), 0)
    plane_s, pair_g = lax.optimization_barrier((plane_s, pair_g))
    plane_g = jnp.sum(exchange(pair_g, ("x", "y")), 0).reshape(2, 96, LANES)

    place = kind * 4 + l

    def along_z(value, k):
        pairs = [((z % 4) * 2 + z // 4, ((z + k) % 8 % 4) * 2 + (z + k) % 8 // 4) for z in range(8)]
        return lax.ppermute(value, ("l", "h"), pairs)

    far = (4, 3, 5, 2, 6, 1, 7)
    rooted = jnp.concatenate([plane_s, root])
    got = [(rooted, place)] + [(along_z(rooted, k), (place - k) % 8) for k in far]
    root_here = sum(jnp.where(source == part, value[96:], 0.0) for value, source in got)
    scale = 1.0 / math.sqrt(atoms * n_dev / configs)
    sums = sum(value[:96] for value, _ in got).reshape(12, 8, LANES) * (root_here * scale)
    sums, plane_g = lax.optimization_barrier((sums, plane_g))
    planes = jnp.broadcast_to(plane_g[None], (4, 2, 96, LANES)).reshape(8, 96, LANES)
    grams = jnp.sum(exchange(planes, ("l", "h")), 0)
    bands = needed(grams, x * 4 + part)
    spread = jnp.concatenate([bands, jnp.broadcast_to(sums.reshape(1, 96, LANES), (4, 96, LANES))], 1)
    spread = jnp.broadcast_to(spread[None], (4, 4, 144, LANES)).reshape(16, 144, LANES)
    mine = exchange(spread, ("x", "y"))
    band = 2 * width // 8
    norm = atoms * n_dev // 8
    normal, rows = call(
        lambda *refs: final_kernel(norm, *refs),
        [jax.ShapeDtypeStruct((band, 2 * width), f32), jax.ShapeDtypeStruct((cfg_here, band), f32)],
        [pos, mine, lax.ppermute(mine, "c", flip), root],
        [
            pltpu.VMEM((configs, 2 * width), f32),
            pltpu.VMEM((configs, band), f32),
            pltpu.VMEM((band, width), f32),
        ],
        pltpu.VMEM,
        24 << 20,
        8 * band * width * configs,
    )
    return normal, rows


def solution(mesh):
    fine = Mesh(mesh.devices.reshape(SIZES), AXES)
    return jax.shard_map(
        shards,
        mesh=fine,
        in_specs=(P(AXES, None), P(AXES), P(AXES), P(), P(("x", "l", "c"))),
        out_specs=(P(("h", "y"), None), P(("x", "l", "c"), ("h", "y"))),
        check_vma=False,
    )
```

```python
import math

import jax
import jax.numpy as jnp
from jax import lax
from jax.experimental import pallas as pl
from jax.experimental.pallas import tpu as pltpu
from jax.sharding import Mesh, PartitionSpec as P

AXES = ("x", "l", "c", "h", "y")
SIZES = (4, 4, 2, 2, 4)
TILE = 256
LANES = 128
PAIRS = ((0, 1), (0, 2), (1, 2), (0, 0), (1, 1), (2, 2))


def put(core, block, first, keep_ref, send_refs):
    for half in range(block.shape[1] // LANES):
        tile = block[:, half * LANES : (half + 1) * LANES].reshape(16, 2, 8, LANES)
        which, at = divmod((first + half) * 8, send_refs[0].shape[1])
        keep_ref[:, (first + half) * 8 : (first + half + 1) * 8, :] = jnp.where(core == 0, tile[:, 0], tile[:, 1])
        send_refs[which][:, at : at + 8, :] = jnp.where(core == 0, tile[:, 1], tile[:, 0])


def load(small, desc_hbm, desc_ref, sems):
    copies = [pltpu.make_async_copy(a, b, sems.at[k]) for k, (a, b) in enumerate(small)]
    for i in range(3):
        cols = slice(i * TILE, (i + 1) * TILE)
        copies.append(pltpu.make_async_copy(desc_hbm.at[:, cols], desc_ref.at[:, cols], sems.at[3 + i]))
    for copy in copies:
        copy.start()
    for copy in copies[:-3]:
        copy.wait()
    return copies[-3:]


def sums_kernel(
    core_ref,
    desc_hbm,
    species_hbm,
    cfg_hbm,
    slot_hbm,
    keep_ref,
    send_ref,
    desc_ref,
    species_ref,
    cfg_ref,
    slot_ref,
    sems,
):
    core = core_ref[0]
    atoms = desc_ref.shape[0]
    configs = slot_ref.shape[1]
    small = ((cfg_hbm, cfg_ref), (slot_hbm, slot_ref), (species_hbm, species_ref))
    blocks = load(small, desc_hbm, desc_ref, sems)
    ids = lax.broadcasted_iota(jnp.int32, (configs, atoms), 0)
    member = (cfg_ref[...] == ids).astype(jnp.bfloat16)
    rows = lax.broadcasted_iota(jnp.int32, (configs, configs), 0)
    place = (slot_ref[...] == rows).astype(jnp.bfloat16)
    placed = jnp.dot(place, member, preferred_element_type=jnp.float32).astype(jnp.bfloat16)
    members = [placed * (species_ref[...] == kind).astype(jnp.bfloat16) for kind in range(2)]
    for j in range(3):
        blocks[j].wait()
        right = desc_ref[:, j * TILE : (j + 1) * TILE]
        for kind in range(2):
            block = jnp.dot(members[kind], right, preferred_element_type=jnp.float32)
            put(core, block, kind * 6 + j * 2, keep_ref, [send_ref])


def gram_kernel(core_ref, desc_hbm, species_hbm, keep_ref, *refs):
    send_refs, (desc_ref, species_ref, turned, sems) = refs[:-4], refs[-4:]
    core = core_ref[0]
    blocks = load(((species_hbm, species_ref),), desc_hbm, desc_ref, sems)
    masks = [(species_ref[...] == kind).astype(jnp.bfloat16) for kind in range(2)]
    for j in range(3):
        blocks[j].wait()
        right = desc_ref[:, j * TILE : (j + 1) * TILE]
        turned[j * TILE : (j + 1) * TILE, :] = right.T
        for i in range(j + 1):
            for kind in range(2):
                left = turned[i * TILE : (i + 1) * TILE, :] * masks[kind]
                block = jnp.dot(left, right, preferred_element_type=jnp.float32)
                put(core, block, kind * 12 + PAIRS.index((i, j)) * 2, keep_ref, send_refs)


def final_kernel(norm, pos_ref, mine_ref, other_ref, root_ref, normal_ref, cfg_ref, full, left, gram):
    core, kind, part, owner = pos_ref[0], pos_ref[1], pos_ref[2], pos_ref[3]
    width = gram.shape[1]
    band = left.shape[1]

    def joined(tile, lo=0, hi=16):
        at = slice(tile * 8, (tile + 1) * 8)
        a, b = mine_ref[lo:hi, at, :], other_ref[lo:hi, at, :]
        pair = [jnp.where(core == which, a, b)[:, None] for which in range(2)]
        return jnp.concatenate(pair, 1).reshape((hi - lo) * 16, LANES)

    for j in range(2 * width // LANES):
        full[:, j * LANES : (j + 1) * LANES] = joined(6 + j)

    def fill(row, col, piece):
        gram[row : row + piece.shape[0], col : col + piece.shape[1]] = piece

    def straight(tiles, lo, hi, row, col):
        for k, tile in enumerate(tiles):
            fill(row, col + k * LANES, joined(tile, lo, hi))

    def band_0():
        straight((4, 5, 0, 1, 2, 3), 0, 12, 0, 0)

    def band_1():
        straight((2, 3, 0, 1, 4, 5), 12, 16, 0, 0)
        fill(64, 0, joined(0).T)
        straight((1, 2, 3, 4), 0, 8, 64, TILE)

    def band_2():
        fill(0, 0, joined(0).T)
        straight((4, 5, 2, 3), 8, 16, 0, TILE)
        fill(128, 0, joined(1).T[:64])
        fill(128, TILE, joined(2).T[:64])
        straight((3, 4), 0, 4, 128, 2 * TILE)

    def band_3():
        fill(0, 0, joined(0).T[64:])
        fill(64, 0, joined(1).T)
        fill(0, TILE, joined(2).T[64:])
        fill(64, TILE, joined(3).T)
        straight((4, 5), 4, 16, 0, 2 * TILE)

    for k, body in enumerate((band_0, band_1, band_2, band_3)):

        @pl.when(part == k)
        def _():
            cols = slice(k * band, (k + 1) * band)
            shifted = slice(width + k * band, width + (k + 1) * band)
            left[...] = jnp.where(kind == 0, full[:, cols], full[:, shifted])
            own = pl.ds(pl.multiple_of(owner * 8, 8), 8)
            tile = jnp.where(kind == 0, full[own, cols], full[own, shifted])
            cfg_ref[...] = tile / root_ref[:, :1]
            body()

    for s in range(2):
        cols = slice(s * width, (s + 1) * width)
        cross = lax.dot_general(
            left[...],
            full[:, cols],
            (((0,), (0,)), ((), ())),
            precision=lax.Precision.HIGHEST,
            preferred_element_type=jnp.float32,
        )
        extra = jnp.where(kind == s, gram[...] * (1.0 / norm), 0.0)
        normal_ref[:, cols] = cross * (1.0 / full.shape[0]) + extra


def call(kernel, outs, args, scratch, space, limit, flops):
    smem = pl.BlockSpec(memory_space=pltpu.SMEM)
    held = [pltpu.with_memory_space_constraint(a, space) for a in args[1:]]
    return pl.pallas_call(
        kernel,
        out_shape=outs,
        in_specs=[smem] + [pl.BlockSpec(memory_space=space)] * len(held),
        out_specs=[pl.BlockSpec(memory_space=pltpu.VMEM)] * len(outs),
        scratch_shapes=list(scratch),
        compiler_params=pltpu.CompilerParams(vmem_limit_bytes=limit),
        cost_estimate=pl.CostEstimate(flops=flops, bytes_accessed=8 << 20, transcendentals=0),
    )(args[0], *held)


def exchange(values, axes):
    flat = values.reshape(-1, values.shape[-1])
    return lax.all_to_all(flat, axes, 0, 0, tiled=True).reshape(values.shape)


def needed(grams, owner):
    def pick(*tiles):
        return jnp.concatenate([grams[8 * k : 8 * k + 8] for k in tiles])

    band_1 = jnp.where(owner >= 12, pick(1, 6, 7, 2, 3), pick(8, 9, 4, 5, 5))
    band_2 = jnp.where(owner >= 8, pick(5, 8, 9), pick(10, 11, 11))
    return jnp.stack(
        [
            pick(0, 1, 2, 3, 6, 7),
            jnp.concatenate([pick(0), band_1]),
            jnp.concatenate([pick(1, 2, 4), band_2]),
            pick(2, 3, 4, 5, 10, 11),
        ]
    )


def shards(desc, species, atom_cfg, slot, weights):
    atoms, width = desc.shape
    configs = slot.shape[0]
    cfg_here = weights.shape[0]
    n_dev = math.prod(SIZES)
    x, l, core, kind, part = [lax.axis_index(axis) for axis in AXES]
    f32 = jnp.float32

    root = jnp.broadcast_to(jnp.sqrt(weights)[:, None], (cfg_here, LANES))
    pos = jnp.stack([core, kind, part, (x * 4 + l) * 2 + core])

    flip = [(0, 1), (1, 0)]
    int_row = pltpu.VMEM((1, atoms), jnp.int32)
    matrix = pltpu.VMEM((atoms, width), jnp.bfloat16)
    sems = pltpu.SemaphoreType.DMA((6,))

    def tiles(count):
        return pltpu.VMEM((16, count * 8, LANES), f32)

    keep_s, send_s = call(
        sums_kernel,
        [tiles(12)] * 2,
        [core[None], desc, species[None], atom_cfg[None], slot[None]],
        [matrix, int_row, int_row, pltpu.VMEM((1, configs), jnp.int32), sems],
        pltpu.HBM,
        24 << 20,
        4 * configs * atoms * width,
    )
    pair_s, desc, pos, root = lax.optimization_barrier((keep_s + lax.ppermute(send_s, "c", flip), desc, pos, root))
    keep_g, *send_g = call(
        gram_kernel,
        [tiles(24)] + [tiles(6)] * 4,
        [core[None], desc, species[None]],
        [matrix, int_row, pltpu.VMEM((width, atoms), jnp.bfloat16), sems],
        pltpu.HBM,
        24 << 20,
        4 * width * width * atoms,
    )
    pair_g = keep_g + jnp.concatenate([lax.ppermute(part_g, "c", flip) for part_g in send_g], 1)
    plane_s = jnp.sum(exchange(pair_s, ("x", "y")), 0)
    plane_s, pair_g = lax.optimization_barrier((plane_s, pair_g))
    plane_g = jnp.sum(exchange(pair_g, ("x", "y")), 0).reshape(2, 96, LANES)

    plane_s = plane_s + lax.ppermute(plane_s, "h", flip)
    rooted = jnp.concatenate([plane_s, root])
    got = [(rooted, l)]
    for k in (2, 1, 3):
        got.append((lax.ppermute(rooted, "l", [(i, (i + k) % 4) for i in range(4)]), (l - k) % 4))
    root_here = sum(jnp.where(source == part, value[96:], 0.0) for value, source in got)
    scale = 1.0 / math.sqrt(atoms * n_dev / configs)
    sums = sum(value[:96] for value, _ in got).reshape(12, 8, LANES) * (root_here * scale)
    sums, plane_g = lax.optimization_barrier((sums, plane_g))
    planes = jnp.broadcast_to(plane_g[None], (4, 2, 96, LANES)).reshape(8, 96, LANES)
    grams = jnp.sum(exchange(planes, ("l", "h")), 0)
    bands = needed(grams, x * 4 + part)
    spread = jnp.concatenate([bands, jnp.broadcast_to(sums.reshape(1, 96, LANES), (4, 96, LANES))], 1)
    spread = jnp.broadcast_to(spread[None], (4, 4, 144, LANES)).reshape(16, 144, LANES)
    mine = exchange(spread, ("x", "y"))
    band = 2 * width // 8
    norm = atoms * n_dev // 8
    normal, rows = call(
        lambda *refs: final_kernel(norm, *refs),
        [jax.ShapeDtypeStruct((band, 2 * width), f32), jax.ShapeDtypeStruct((cfg_here, band), f32)],
        [pos, mine, lax.ppermute(mine, "c", flip), root],
        [
            pltpu.VMEM((configs, 2 * width), f32),
            pltpu.VMEM((configs, band), f32),
            pltpu.VMEM((band, width), f32),
        ],
        pltpu.VMEM,
        24 << 20,
        8 * band * width * configs,
    )
    return normal, rows


def solution(mesh):
    fine = Mesh(mesh.devices.reshape(SIZES), AXES)
    return jax.shard_map(
        shards,
        mesh=fine,
        in_specs=(P(AXES, None), P(AXES), P(AXES), P(), P(("x", "l", "c"))),
        out_specs=(P(("h", "y"), None), P(("x", "l", "c"), ("h", "y"))),
        check_vma=False,
    )
```

```python
import math

import jax
import jax.numpy as jnp
from jax import lax
from jax.experimental import pallas as pl
from jax.experimental.pallas import tpu as pltpu
from jax.sharding import Mesh, PartitionSpec as P

AXES = ("x", "l", "c", "h", "y")
SIZES = (4, 4, 2, 2, 4)
TILE = 256
LANES = 128
PAIRS = ((0, 1), (0, 2), (1, 2))


def put(core, tile, index, keep_ref, send_refs, owner=0):
    tile = tile.reshape(-1, 2, 8, LANES)
    owners = slice(owner, owner + tile.shape[0])
    which, at = divmod(index * 8, send_refs[0].shape[1])
    keep_ref[owners, index * 8 : index * 8 + 8, :] = jnp.where(core == 0, tile[:, 0], tile[:, 1])
    send_refs[which][owners, at : at + 8, :] = jnp.where(core == 0, tile[:, 1], tile[:, 0])


def load(small, desc_hbm, desc_ref, sems):
    copies = [pltpu.make_async_copy(a, b, sems.at[k]) for k, (a, b) in enumerate(small)]
    for i in range(3):
        cols = slice(i * TILE, (i + 1) * TILE)
        copies.append(pltpu.make_async_copy(desc_hbm.at[:, cols], desc_ref.at[:, cols], sems.at[3 + i]))
    for copy in copies:
        copy.start()
    for copy in copies[:-3]:
        copy.wait()
    return copies[-3:]


def sums_kernel(
    core_ref,
    desc_hbm,
    species_hbm,
    cfg_hbm,
    slot_hbm,
    keep_ref,
    send_ref,
    desc_ref,
    species_ref,
    cfg_ref,
    slot_ref,
    sems,
):
    core = core_ref[0]
    atoms = desc_ref.shape[0]
    configs = slot_ref.shape[1]
    small = ((cfg_hbm, cfg_ref), (slot_hbm, slot_ref), (species_hbm, species_ref))
    blocks = load(small, desc_hbm, desc_ref, sems)
    ids = lax.broadcasted_iota(jnp.int32, (configs, atoms), 0)
    member = (cfg_ref[...] == ids).astype(jnp.bfloat16)
    rows = lax.broadcasted_iota(jnp.int32, (configs, configs), 0)
    place = (slot_ref[...] == rows).astype(jnp.bfloat16)
    placed = jnp.dot(place, member, preferred_element_type=jnp.float32).astype(jnp.bfloat16)
    members = [placed * (species_ref[...] == kind).astype(jnp.bfloat16) for kind in range(2)]
    for j in range(3):
        blocks[j].wait()
        right = desc_ref[:, j * TILE : (j + 1) * TILE]
        for kind in range(2):
            block = jnp.dot(members[kind], right, preferred_element_type=jnp.float32)
            for half in range(2):
                tile = block[:, half * LANES : (half + 1) * LANES]
                put(core, tile, kind * 6 + j * 2 + half, keep_ref, [send_ref])


def gram_kernel(core_ref, desc_hbm, species_hbm, keep_ref, *refs):
    send_refs, (desc_ref, species_ref, turned, sems) = refs[:-4], refs[-4:]
    core = core_ref[0]
    blocks = load(((species_hbm, species_ref),), desc_hbm, desc_ref, sems)
    masks = [(species_ref[...] == kind).astype(jnp.bfloat16) for kind in range(2)]
    for j in range(3):
        blocks[j].wait()
        right = desc_ref[:, j * TILE : (j + 1) * TILE]
        turned[j * TILE : (j + 1) * TILE, :] = right.T
        for i in range(j + 1):
            for kind in range(2):
                left = turned[i * TILE : (i + 1) * TILE, :] * masks[kind]
                block = jnp.dot(left, right, preferred_element_type=jnp.float32)
                if i == j:
                    put(core, block[:LANES, :LANES], 18 + i, keep_ref, send_refs, 8 * kind)
                    put(core, block[:, LANES:], kind * 9 + 6 + i, keep_ref, send_refs)
                else:
                    first = kind * 9 + PAIRS.index((i, j)) * 2
                    put(core, block[:, :LANES], first, keep_ref, send_refs)
                    put(core, block[:, LANES:], first + 1, keep_ref, send_refs)


def final_kernel(norm, pos_ref, mine_ref, other_ref, root_ref, normal_ref, cfg_ref, full, left, gram):
    core, kind, part, owner = pos_ref[0], pos_ref[1], pos_ref[2], pos_ref[3]
    width = gram.shape[1]
    band = left.shape[1]

    def joined(tile, lo=0, hi=16):
        at = slice(tile * 8, (tile + 1) * 8)
        a, b = mine_ref[lo:hi, at, :], other_ref[lo:hi, at, :]
        pair = [jnp.where(core == which, a, b)[:, None] for which in range(2)]
        return jnp.concatenate(pair, 1).reshape((hi - lo) * 16, LANES)

    for j in range(2 * width // LANES):
        full[:, j * LANES : (j + 1) * LANES] = joined(6 + j)

    def fill(row, col, piece):
        gram[row : row + piece.shape[0], col : col + piece.shape[1]] = piece

    def straight(tiles, lo, hi, row, col):
        for k, tile in enumerate(tiles):
            fill(row, col + k * LANES, joined(tile, lo, hi))

    def corner():
        return jnp.where(kind == 0, joined(5, 0, 8), joined(5, 8, 16))

    def band_0():
        fill(0, 0, corner())
        fill(128, 0, joined(4, 0, 8).T[:64])
        straight((4, 0, 1, 2, 3), 0, 12, 0, LANES)

    def band_1():
        fill(0, 0, joined(4, 0, 8).T[64:])
        straight((4, 0, 1, 2, 3), 12, 16, 0, LANES)
        fill(64, 0, joined(0).T)
        fill(64, TILE, corner())
        straight((1, 2, 3), 0, 8, 64, TILE + LANES)

    def band_2():
        fill(0, 0, joined(0).T)
        fill(0, TILE, joined(3, 0, 8).T)
        straight((3, 2, 4), 8, 16, 0, TILE + LANES)
        fill(128, 0, joined(1).T[:64])
        fill(128, TILE, joined(2).T[:64])
        fill(128, 2 * TILE, corner()[:64])
        straight((4,), 0, 4, 128, 2 * TILE + LANES)

    def band_3():
        fill(0, 0, joined(0).T[64:])
        fill(64, 0, joined(1).T)
        fill(0, TILE, joined(2).T[64:])
        fill(64, TILE, joined(3).T)
        fill(0, 2 * TILE, corner()[64:])
        fill(64, 2 * TILE, joined(4, 0, 8).T)
        straight((4,), 4, 16, 0, 2 * TILE + LANES)

    for k, body in enumerate((band_0, band_1, band_2, band_3)):

        @pl.when(part == k)
        def _():
            cols = slice(k * band, (k + 1) * band)
            shifted = slice(width + k * band, width + (k + 1) * band)
            left[...] = jnp.where(kind == 0, full[:, cols], full[:, shifted])
            own = pl.ds(pl.multiple_of(owner * 8, 8), 8)
            tile = jnp.where(kind == 0, full[own, cols], full[own, shifted])
            cfg_ref[...] = tile / root_ref[:, :1]
            body()

    for s in range(2):
        cols = slice(s * width, (s + 1) * width)
        cross = lax.dot_general(
            left[...],
            full[:, cols],
            (((0,), (0,)), ((), ())),
            precision=lax.Precision.HIGHEST,
            preferred_element_type=jnp.float32,
        )
        extra = jnp.where(kind == s, gram[...] * (1.0 / norm), 0.0)
        normal_ref[:, cols] = cross * (1.0 / full.shape[0]) + extra


def call(kernel, outs, args, scratch, space, limit, flops):
    smem = pl.BlockSpec(memory_space=pltpu.SMEM)
    held = [pltpu.with_memory_space_constraint(a, space) for a in args[1:]]
    return pl.pallas_call(
        kernel,
        out_shape=outs,
        in_specs=[smem] + [pl.BlockSpec(memory_space=space)] * len(held),
        out_specs=[pl.BlockSpec(memory_space=pltpu.VMEM)] * len(outs),
        scratch_shapes=list(scratch),
        compiler_params=pltpu.CompilerParams(vmem_limit_bytes=limit),
        cost_estimate=pl.CostEstimate(flops=flops, bytes_accessed=8 << 20, transcendentals=0),
    )(args[0], *held)


def exchange(values, axes):
    flat = values.reshape(-1, values.shape[-1])
    return lax.all_to_all(flat, axes, 0, 0, tiled=True).reshape(values.shape)


def needed(grams, owner):
    def pick(*tiles):
        return jnp.concatenate([grams[8 * k : 8 * k + 8] for k in tiles])

    band_1 = jnp.where(owner >= 12, pick(1, 2, 3), pick(7, 4, 5))
    band_2 = jnp.where(owner >= 8, pick(5), pick(8))
    return jnp.stack(
        [
            pick(0, 1, 2, 3, 6, 9),
            jnp.concatenate([pick(0), band_1, pick(6, 10)]),
            jnp.concatenate([pick(1, 2, 4, 7), band_2, pick(11)]),
            pick(2, 3, 4, 5, 8, 11),
        ]
    )


def shards(desc, species, atom_cfg, slot, weights):
    atoms, width = desc.shape
    configs = slot.shape[0]
    cfg_here = weights.shape[0]
    n_dev = math.prod(SIZES)
    x, l, core, kind, part = [lax.axis_index(axis) for axis in AXES]
    f32 = jnp.float32

    root = jnp.broadcast_to(jnp.sqrt(weights)[:, None], (cfg_here, LANES))
    pos = jnp.stack([core, kind, part, (x * 4 + l) * 2 + core])

    flip = [(0, 1), (1, 0)]
    int_row = pltpu.VMEM((1, atoms), jnp.int32)
    matrix = pltpu.VMEM((atoms, width), jnp.bfloat16)
    sems = pltpu.SemaphoreType.DMA((6,))

    def tiles(count):
        return pltpu.VMEM((16, count * 8, LANES), f32)

    keep_s, send_s = call(
        sums_kernel,
        [tiles(12)] * 2,
        [core[None], desc, species[None], atom_cfg[None], slot[None]],
        [matrix, int_row, int_row, pltpu.VMEM((1, configs), jnp.int32), sems],
        pltpu.HBM,
        24 << 20,
        4 * configs * atoms * width,
    )
    pair_s, desc, pos, root = lax.optimization_barrier((keep_s + lax.ppermute(send_s, "c", flip), desc, pos, root))
    keep_g, *send_g = call(
        gram_kernel,
        [tiles(21)] + [tiles(6)] * 3 + [tiles(3)],
        [core[None], desc, species[None]],
        [matrix, int_row, pltpu.VMEM((width, atoms), jnp.bfloat16), sems],
        pltpu.HBM,
        24 << 20,
        4 * width * width * atoms,
    )
    pair_g = keep_g + jnp.concatenate([lax.ppermute(part_g, "c", flip) for part_g in send_g], 1)
    plane_s = jnp.sum(exchange(pair_s, ("x", "y")), 0)
    plane_s, pair_g = lax.optimization_barrier((plane_s, pair_g))
    plane_g = jnp.sum(exchange(pair_g, ("x", "y")), 0)

    plane_s = plane_s + lax.ppermute(plane_s, "h", flip)
    rooted = jnp.concatenate([plane_s, root])
    got = [(rooted, l)]
    for k in (2, 1, 3):
        got.append((lax.ppermute(rooted, "l", [(i, (i + k) % 4) for i in range(4)]), (l - k) % 4))
    root_here = sum(jnp.where(source == part, value[96:], 0.0) for value, source in got)
    scale = 1.0 / math.sqrt(atoms * n_dev / configs)
    sums = sum(value[:96] for value, _ in got).reshape(12, 8, LANES) * (root_here * scale)
    sums, plane_g = lax.optimization_barrier((sums, plane_g))
    corner = jnp.broadcast_to(plane_g[None, 144:], (2, 24, LANES))
    planes = jnp.concatenate([plane_g[:144].reshape(2, 72, LANES), corner], 1)
    planes = jnp.broadcast_to(planes[None], (4, 2, 96, LANES)).reshape(8, 96, LANES)
    grams = jnp.sum(exchange(planes, ("l", "h")), 0)
    bands = needed(grams, x * 4 + part)
    spread = jnp.concatenate([bands, jnp.broadcast_to(sums.reshape(1, 96, LANES), (4, 96, LANES))], 1)
    spread = jnp.broadcast_to(spread[None], (4, 4, 144, LANES)).reshape(16, 144, LANES)
    mine = exchange(spread, ("x", "y"))
    band = 2 * width // 8
    norm = atoms * n_dev // 8
    normal, rows = call(
        lambda *refs: final_kernel(norm, *refs),
        [jax.ShapeDtypeStruct((band, 2 * width), f32), jax.ShapeDtypeStruct((cfg_here, band), f32)],
        [pos, mine, lax.ppermute(mine, "c", flip), root],
        [
            pltpu.VMEM((configs, 2 * width), f32),
            pltpu.VMEM((configs, band), f32),
            pltpu.VMEM((band, width), f32),
        ],
        pltpu.VMEM,
        24 << 20,
        8 * band * width * configs,
    )
    return normal, rows


def solution(mesh):
    fine = Mesh(mesh.devices.reshape(SIZES), AXES)
    return jax.shard_map(
        shards,
        mesh=fine,
        in_specs=(P(AXES, None), P(AXES), P(AXES), P(), P(("x", "l", "c"))),
        out_specs=(P(("h", "y"), None), P(("x", "l", "c"), ("h", "y"))),
        check_vma=False,
    )
```

```python
import functools
import math

import jax
import jax.numpy as jnp
from jax import lax
from jax.experimental import pallas as pl
from jax.experimental.pallas import tpu as pltpu
from jax.sharding import Mesh, PartitionSpec as P

AXES = ("x", "l", "c", "h", "y")
SIZES = (4, 4, 2, 2, 4)
TILE = 256
LANES = 128
PAIRS = ((0, 1), (0, 2), (1, 2))


def put(core, tile, index, keep_ref, send_refs, owner=0):
    tile = tile.reshape(-1, 2, 8, LANES)
    owners = slice(owner, owner + tile.shape[0])
    which, at = divmod(index * 8, send_refs[0].shape[1])
    keep_ref[owners, index * 8 : index * 8 + 8, :] = jnp.where(core == 0, tile[:, 0], tile[:, 1])
    send_refs[which][owners, at : at + 8, :] = jnp.where(core == 0, tile[:, 1], tile[:, 0])


def load(small, desc_hbm, desc_ref, sems):
    copies = [pltpu.make_async_copy(a, b, sems.at[k]) for k, (a, b) in enumerate(small)]
    for i in range(3):
        cols = slice(i * TILE, (i + 1) * TILE)
        copies.append(pltpu.make_async_copy(desc_hbm.at[:, cols], desc_ref.at[:, cols], sems.at[3 + i]))
    for copy in copies:
        copy.start()
    for copy in copies[:-3]:
        copy.wait()
    return copies[-3:]


def sums_kernel(
    core_ref,
    desc_hbm,
    species_hbm,
    cfg_hbm,
    slot_hbm,
    keep_ref,
    send_ref,
    desc_ref,
    species_ref,
    cfg_ref,
    slot_ref,
    sems,
):
    core = core_ref[0]
    atoms = desc_ref.shape[0]
    configs = slot_ref.shape[1]
    small = ((cfg_hbm, cfg_ref), (slot_hbm, slot_ref), (species_hbm, species_ref))
    blocks = load(small, desc_hbm, desc_ref, sems)
    ids = lax.broadcasted_iota(jnp.int32, (configs, atoms), 0)
    member = (cfg_ref[...] == ids).astype(jnp.bfloat16)
    rows = lax.broadcasted_iota(jnp.int32, (configs, configs), 0)
    place = (slot_ref[...] == rows).astype(jnp.bfloat16)
    placed = jnp.dot(place, member, preferred_element_type=jnp.float32).astype(jnp.bfloat16)
    members = [placed * (species_ref[...] == kind).astype(jnp.bfloat16) for kind in range(2)]
    for j in range(3):
        blocks[j].wait()
        right = desc_ref[:, j * TILE : (j + 1) * TILE]
        for kind in range(2):
            block = jnp.dot(members[kind], right, preferred_element_type=jnp.float32)
            for half in range(2):
                tile = block[:, half * LANES : (half + 1) * LANES]
                put(core, tile, kind * 6 + j * 2 + half, keep_ref, [send_ref])


def gram_kernel(core_ref, desc_hbm, species_hbm, keep_ref, *refs):
    send_refs, (desc_ref, species_ref, turned, sems) = refs[:-4], refs[-4:]
    core = core_ref[0]
    blocks = load(((species_hbm, species_ref),), desc_hbm, desc_ref, sems)
    masks = [(species_ref[...] == kind).astype(jnp.bfloat16) for kind in range(2)]
    for j in range(3):
        blocks[j].wait()
        right = desc_ref[:, j * TILE : (j + 1) * TILE]
        turned[j * TILE : (j + 1) * TILE, :] = right.T
        for i in range(j + 1):
            for kind in range(2):
                left = turned[i * TILE : (i + 1) * TILE, :] * masks[kind]
                block = jnp.dot(left, right, preferred_element_type=jnp.float32)
                if i == j:
                    put(core, block[:LANES, :LANES], 18 + i, keep_ref, send_refs, 8 * kind)
                    put(core, block[:, LANES:], kind * 9 + 6 + i, keep_ref, send_refs)
                else:
                    first = kind * 9 + PAIRS.index((i, j)) * 2
                    put(core, block[:, :LANES], first, keep_ref, send_refs)
                    put(core, block[:, LANES:], first + 1, keep_ref, send_refs)


def joined_rows(core, refs, tile, lo=0, hi=16):
    at = slice(tile * 8, (tile + 1) * 8)
    a, b = [ref[lo:hi, at, :] for ref in refs]
    pair = [jnp.where(core == which, a, b)[:, None] for which in range(2)]
    return jnp.concatenate(pair, 1).reshape((hi - lo) * 16, LANES)


def product_kernel(pos_ref, mine_ref, other_ref, root_ref, cross_ref, cfg_ref, full, left):
    core, kind, part, owner = pos_ref[0], pos_ref[1], pos_ref[2], pos_ref[3]
    width = full.shape[1] // 2
    band = left.shape[1]
    for j in range(2 * width // LANES):
        full[:, j * LANES : (j + 1) * LANES] = joined_rows(core, (mine_ref, other_ref), j)
    for k in range(4):

        @pl.when(part == k)
        def _():
            cols = slice(k * band, (k + 1) * band)
            shifted = slice(width + k * band, width + (k + 1) * band)
            left[...] = jnp.where(kind == 0, full[:, cols], full[:, shifted])
            own = pl.ds(pl.multiple_of(owner * 8, 8), 8)
            tile = jnp.where(kind == 0, full[own, cols], full[own, shifted])
            cfg_ref[...] = tile / root_ref[:, :1]

    cross = lax.dot_general(
        left[...],
        full[...],
        (((0,), (0,)), ((), ())),
        precision=lax.Precision.HIGHEST,
        preferred_element_type=jnp.float32,
    )
    cross_ref[...] = cross * (1.0 / full.shape[0])


def final_kernel(norm, pos_ref, mine_ref, other_ref, cross_ref, normal_ref, gram):
    core, kind, part = pos_ref[0], pos_ref[1], pos_ref[2]
    width = gram.shape[1]

    def joined(tile, lo=0, hi=16):
        return joined_rows(core, (mine_ref, other_ref), tile, lo, hi)

    def fill(row, col, piece):
        gram[row : row + piece.shape[0], col : col + piece.shape[1]] = piece

    def straight(tiles, lo, hi, row, col):
        for k, tile in enumerate(tiles):
            fill(row, col + k * LANES, joined(tile, lo, hi))

    def corner():
        return jnp.where(kind == 0, joined(5, 0, 8), joined(5, 8, 16))

    def band_0():
        fill(0, 0, corner())
        fill(128, 0, joined(4, 0, 8).T[:64])
        straight((4, 0, 1, 2, 3), 0, 12, 0, LANES)

    def band_1():
        fill(0, 0, joined(4, 0, 8).T[64:])
        straight((4, 0, 1, 2, 3), 12, 16, 0, LANES)
        fill(64, 0, joined(0).T)
        fill(64, TILE, corner())
        straight((1, 2, 3), 0, 8, 64, TILE + LANES)

    def band_2():
        fill(0, 0, joined(0).T)
        fill(0, TILE, joined(3, 0, 8).T)
        straight((3, 2, 4), 8, 16, 0, TILE + LANES)
        fill(128, 0, joined(1).T[:64])
        fill(128, TILE, joined(2).T[:64])
        fill(128, 2 * TILE, corner()[:64])
        straight((4,), 0, 4, 128, 2 * TILE + LANES)

    def band_3():
        fill(0, 0, joined(0).T[64:])
        fill(64, 0, joined(1).T)
        fill(0, TILE, joined(2).T[64:])
        fill(64, TILE, joined(3).T)
        fill(0, 2 * TILE, corner()[64:])
        fill(64, 2 * TILE, joined(4, 0, 8).T)
        straight((4,), 4, 16, 0, 2 * TILE + LANES)

    for k, body in enumerate((band_0, band_1, band_2, band_3)):
        pl.when(part == k)(body)

    for which in range(2):
        cols = slice(which * width, (which + 1) * width)
        extra = jnp.where(kind == which, gram[...] * (1.0 / norm), 0.0)
        normal_ref[:, cols] = cross_ref[:, cols] + extra


def call(kernel, outs, args, scratch, space, limit, flops):
    smem = pl.BlockSpec(memory_space=pltpu.SMEM)
    held = [pltpu.with_memory_space_constraint(a, space) for a in args[1:]]
    return pl.pallas_call(
        kernel,
        out_shape=outs,
        in_specs=[smem] + [pl.BlockSpec(memory_space=space)] * len(held),
        out_specs=[pl.BlockSpec(memory_space=pltpu.VMEM)] * len(outs),
        scratch_shapes=list(scratch),
        compiler_params=pltpu.CompilerParams(vmem_limit_bytes=limit),
        cost_estimate=pl.CostEstimate(flops=flops, bytes_accessed=flops >> 9, transcendentals=0),
    )(args[0], *held)


def exchange(values, axes):
    flat = values.reshape(-1, values.shape[-1])
    return lax.all_to_all(flat, axes, 0, 0, tiled=True).reshape(values.shape)


def bands_kernel(owner_ref, *refs):
    owner, out_ref = owner_ref[0], refs[-1]
    total = refs[0][...]
    for ref in refs[1:-1]:
        total = total + ref[...]

    def tile(k):
        return total[8 * k : 8 * k + 8]

    def either(first, a, b):
        return jnp.where(owner >= first, tile(a), tile(b))

    bands = (
        [tile(k) for k in (0, 1, 2, 3, 6, 9)],
        [tile(0), either(12, 1, 7), either(12, 2, 4), either(12, 3, 5), tile(6), tile(10)],
        [tile(1), tile(2), tile(4), tile(7), either(8, 5, 8), tile(11)],
        [tile(k) for k in (2, 3, 4, 5, 8, 11)],
    )
    for k in range(16):
        for at, piece in enumerate(bands[k % 4]):
            out_ref[k, at * 8 : at * 8 + 8, :] = piece


def shards(desc, species, atom_cfg, slot, weights):
    atoms, width = desc.shape
    configs = slot.shape[0]
    cfg_here = weights.shape[0]
    n_dev = math.prod(SIZES)
    x, l, core, kind, part = [lax.axis_index(axis) for axis in AXES]
    f32 = jnp.float32

    root = jnp.broadcast_to(jnp.sqrt(weights)[:, None], (cfg_here, LANES))
    pos = jnp.stack([core, kind, part, (x * 4 + l) * 2 + core])

    flip = [(0, 1), (1, 0)]
    int_row = pltpu.VMEM((1, atoms), jnp.int32)
    matrix = pltpu.VMEM((atoms, width), jnp.bfloat16)
    sems = pltpu.SemaphoreType.DMA((6,))

    def tiles(count):
        return pltpu.VMEM((16, count * 8, LANES), f32)

    keep_s, send_s = call(
        sums_kernel,
        [tiles(12)] * 2,
        [core[None], desc, species[None], atom_cfg[None], slot[None]],
        [matrix, int_row, int_row, pltpu.VMEM((1, configs), jnp.int32), sems],
        pltpu.HBM,
        24 << 20,
        4 * configs * atoms * width,
    )
    pair_s, desc, pos, root = lax.optimization_barrier((keep_s + lax.ppermute(send_s, "c", flip), desc, pos, root))
    keep_g, *send_g = call(
        gram_kernel,
        [tiles(21)] + [tiles(6)] * 3 + [tiles(3)],
        [core[None], desc, species[None]],
        [matrix, int_row, pltpu.VMEM((width, atoms), jnp.bfloat16), sems],
        pltpu.HBM,
        24 << 20,
        4 * width * width * atoms,
    )
    pair_g = keep_g + jnp.concatenate([lax.ppermute(part_g, "c", flip) for part_g in send_g], 1)
    plane_s = jnp.sum(exchange(pair_s, ("x", "y")), 0)
    plane_s, pair_g = lax.optimization_barrier((plane_s, pair_g))
    plane_g = jnp.sum(exchange(pair_g, ("x", "y")), 0)

    def along_l(value, k):
        return lax.ppermute(value, "l", [(i, (i + k) % 4) for i in range(4)])

    plane_s = plane_s + lax.ppermute(plane_s, "h", flip)
    rooted = jnp.concatenate([plane_s, root])
    got = [(rooted, l)]
    for k in (2, 1, 3):
        got.append((along_l(rooted, k), (l - k) % 4))
    root_here = sum(jnp.where(source == part, value[96:], 0.0) for value, source in got)
    scale = 1.0 / math.sqrt(atoms * n_dev / configs)
    sums = sum(value[:96] for value, _ in got).reshape(12, 8, LANES) * (root_here * scale)
    sums, plane_g = lax.optimization_barrier((sums, plane_g))
    def of_species(which):
        return jnp.concatenate([lax.dynamic_slice_in_dim(plane_g, which * 72, 72), plane_g[144:]])

    mine_s = exchange(jnp.broadcast_to(sums.reshape(1, 96, LANES), (16, 96, LANES)), ("x", "y"))
    grams = of_species(kind) + lax.ppermute(of_species(1 - kind), "h", flip)
    (spread,) = call(
        bands_kernel,
        [tiles(6)],
        [(x * 4 + part)[None], grams] + [along_l(grams, k) for k in (2, 1, 3)],
        (),
        pltpu.VMEM,
        8 << 20,
        1,
    )
    spread, mine_s = lax.optimization_barrier((spread, mine_s))
    mine_g = exchange(spread, ("x", "y"))
    band = 2 * width // 8
    norm = atoms * n_dev // 8
    cross, rows = call(
        product_kernel,
        [pltpu.VMEM((band, 2 * width), f32), jax.ShapeDtypeStruct((cfg_here, band), f32)],
        [pos, mine_s, lax.ppermute(mine_s, "c", flip), root],
        [pltpu.VMEM((configs, 2 * width), f32), pltpu.VMEM((configs, band), f32)],
        pltpu.VMEM,
        24 << 20,
        24 * band * width * configs,
    )
    (normal,) = call(
        functools.partial(final_kernel, norm),
        [jax.ShapeDtypeStruct((band, 2 * width), f32)],
        [pos, mine_g, lax.ppermute(mine_g, "c", flip), cross],
        [pltpu.VMEM((band, width), f32)],
        pltpu.VMEM,
        24 << 20,
        band * width,
    )
    return normal, rows


def solution(mesh):
    fine = Mesh(mesh.devices.reshape(SIZES), AXES)
    return jax.shard_map(
        shards,
        mesh=fine,
        in_specs=(P(AXES, None), P(AXES), P(AXES), P(), P(("x", "l", "c"))),
        out_specs=(P(("h", "y"), None), P(("x", "l", "c"), ("h", "y"))),
        check_vma=False,
    )
```

```python
import functools
import math

import jax
import jax.numpy as jnp
from jax import lax
from jax.experimental import pallas as pl
from jax.experimental.pallas import tpu as pltpu
from jax.sharding import Mesh, PartitionSpec as P

AXES = ("x", "l", "c", "h", "y")
SIZES = (4, 4, 2, 2, 4)
TILE = 256
LANES = 128
PAIRS = ((0, 1), (0, 2), (1, 2))


def put(core, tile, index, keep_ref, send_refs, owner=0):
    tile = tile.reshape(-1, 2, 8, LANES)
    owners = slice(owner, owner + tile.shape[0])
    which, at = divmod(index * 8, send_refs[0].shape[1])
    keep_ref[owners, index * 8 : index * 8 + 8, :] = jnp.where(core == 0, tile[:, 0], tile[:, 1])
    send_refs[which][owners, at : at + 8, :] = jnp.where(core == 0, tile[:, 1], tile[:, 0])


def load(small, desc_hbm, desc_ref, sems):
    copies = [pltpu.make_async_copy(a, b, sems.at[k]) for k, (a, b) in enumerate(small)]
    for i in range(3):
        cols = slice(i * TILE, (i + 1) * TILE)
        copies.append(pltpu.make_async_copy(desc_hbm.at[:, cols], desc_ref.at[:, cols], sems.at[3 + i]))
    for copy in copies:
        copy.start()
    for copy in copies[:-3]:
        copy.wait()
    return copies[-3:]


def sums_kernel(
    core_ref,
    desc_hbm,
    species_hbm,
    cfg_hbm,
    slot_hbm,
    keep_ref,
    send_ref,
    desc_ref,
    species_ref,
    cfg_ref,
    slot_ref,
    sems,
):
    core = core_ref[0]
    atoms = desc_ref.shape[0]
    configs = slot_ref.shape[1]
    small = ((cfg_hbm, cfg_ref), (slot_hbm, slot_ref), (species_hbm, species_ref))
    blocks = load(small, desc_hbm, desc_ref, sems)
    ids = lax.broadcasted_iota(jnp.int32, (configs, atoms), 0)
    member = (cfg_ref[...] == ids).astype(jnp.bfloat16)
    rows = lax.broadcasted_iota(jnp.int32, (configs, configs), 0)
    place = (slot_ref[...] == rows).astype(jnp.bfloat16)
    placed = jnp.dot(place, member, preferred_element_type=jnp.float32).astype(jnp.bfloat16)
    members = [placed * (species_ref[...] == kind).astype(jnp.bfloat16) for kind in range(2)]
    for j in range(3):
        blocks[j].wait()
        right = desc_ref[:, j * TILE : (j + 1) * TILE]
        for kind in range(2):
            block = jnp.dot(members[kind], right, preferred_element_type=jnp.float32)
            for half in range(2):
                tile = block[:, half * LANES : (half + 1) * LANES]
                put(core, tile, kind * 6 + j * 2 + half, keep_ref, [send_ref])


def gram_kernel(core_ref, desc_hbm, species_hbm, keep_ref, *refs):
    send_refs, (desc_ref, species_ref, turned, sems) = refs[:-4], refs[-4:]
    core = core_ref[0]
    blocks = load(((species_hbm, species_ref),), desc_hbm, desc_ref, sems)
    masks = [(species_ref[...] == kind).astype(jnp.bfloat16) for kind in range(2)]
    for j in range(3):
        blocks[j].wait()
        right = desc_ref[:, j * TILE : (j + 1) * TILE]
        turned[j * TILE : (j + 1) * TILE, :] = right.T
        for i in range(j + 1):
            for kind in range(2):
                left = turned[i * TILE : (i + 1) * TILE, :] * masks[kind]
                block = jnp.dot(left, right, preferred_element_type=jnp.float32)
                if i == j:
                    put(core, block[:LANES, :LANES], 18 + i, keep_ref, send_refs, 8 * kind)
                    put(core, block[:, LANES:], kind * 9 + 6 + i, keep_ref, send_refs)
                else:
                    first = kind * 9 + PAIRS.index((i, j)) * 2
                    put(core, block[:, :LANES], first, keep_ref, send_refs)
                    put(core, block[:, LANES:], first + 1, keep_ref, send_refs)


def joined_rows(core, refs, tile, lo=0, hi=16):
    at = slice(tile * 8, (tile + 1) * 8)
    a, b = [ref[lo:hi, at, :] for ref in refs]
    pair = [jnp.where(core == which, a, b)[:, None] for which in range(2)]
    return jnp.concatenate(pair, 1).reshape((hi - lo) * 16, LANES)


def product_kernel(pos_ref, mine_ref, other_ref, root_ref, cross_ref, cfg_ref, full, left):
    core, kind, part, owner = pos_ref[0], pos_ref[1], pos_ref[2], pos_ref[3]
    width = full.shape[1] // 2
    band = left.shape[1]
    for j in range(2 * width // LANES):
        full[:, j * LANES : (j + 1) * LANES] = joined_rows(core, (mine_ref, other_ref), j)
    for k in range(4):

        @pl.when(part == k)
        def _():
            cols = slice(k * band, (k + 1) * band)
            shifted = slice(width + k * band, width + (k + 1) * band)
            left[...] = jnp.where(kind == 0, full[:, cols], full[:, shifted])
            own = pl.ds(pl.multiple_of(owner * 8, 8), 8)
            tile = jnp.where(kind == 0, full[own, cols], full[own, shifted])
            cfg_ref[...] = tile / root_ref[:, :1]

    cross = lax.dot_general(
        left[...],
        full[...],
        (((0,), (0,)), ((), ())),
        precision=lax.Precision.HIGHEST,
        preferred_element_type=jnp.float32,
    )
    cross_ref[...] = cross * (1.0 / full.shape[0])


def final_kernel(norm, pos_ref, mine_ref, other_ref, cross_ref, normal_ref, gram):
    core, kind, part = pos_ref[0], pos_ref[1], pos_ref[2]
    width = gram.shape[1]

    def joined(tile, lo=0, hi=16):
        return joined_rows(core, (mine_ref, other_ref), tile, lo, hi)

    def fill(row, col, piece):
        gram[row : row + piece.shape[0], col : col + piece.shape[1]] = piece

    def straight(tiles, lo, hi, row, col):
        for k, tile in enumerate(tiles):
            fill(row, col + k * LANES, joined(tile, lo, hi))

    def corner():
        return jnp.where(kind == 0, joined(5, 0, 8), joined(5, 8, 16))

    def band_0():
        fill(0, 0, corner())
        fill(128, 0, joined(4, 0, 8).T[:64])
        straight((4, 0, 1, 2, 3), 0, 12, 0, LANES)

    def band_1():
        fill(0, 0, joined(4, 0, 8).T[64:])
        straight((4, 0, 1, 2, 3), 12, 16, 0, LANES)
        fill(64, 0, joined(0).T)
        fill(64, TILE, corner())
        straight((1, 2, 3), 0, 8, 64, TILE + LANES)

    def band_2():
        fill(0, 0, joined(0).T)
        fill(0, TILE, joined(3, 0, 8).T)
        straight((3, 2, 4), 8, 16, 0, TILE + LANES)
        fill(128, 0, joined(1).T[:64])
        fill(128, TILE, joined(2).T[:64])
        fill(128, 2 * TILE, corner()[:64])
        straight((4,), 0, 4, 128, 2 * TILE + LANES)

    def band_3():
        fill(0, 0, joined(0).T[64:])
        fill(64, 0, joined(1).T)
        fill(0, TILE, joined(2).T[64:])
        fill(64, TILE, joined(3).T)
        fill(0, 2 * TILE, corner()[64:])
        fill(64, 2 * TILE, joined(4, 0, 8).T)
        straight((4,), 4, 16, 0, 2 * TILE + LANES)

    for k, body in enumerate((band_0, band_1, band_2, band_3)):
        pl.when(part == k)(body)

    for which in range(2):
        cols = slice(which * width, (which + 1) * width)
        extra = jnp.where(kind == which, gram[...] * (1.0 / norm), 0.0)
        normal_ref[:, cols] = cross_ref[:, cols] + extra


def call(kernel, outs, args, scratch, space, limit, flops):
    smem = pl.BlockSpec(memory_space=pltpu.SMEM)
    held = [pltpu.with_memory_space_constraint(a, space) for a in args[1:]]
    return pl.pallas_call(
        kernel,
        out_shape=outs,
        in_specs=[smem] + [pl.BlockSpec(memory_space=space)] * len(held),
        out_specs=[pl.BlockSpec(memory_space=pltpu.VMEM)] * len(outs),
        scratch_shapes=list(scratch),
        compiler_params=pltpu.CompilerParams(vmem_limit_bytes=limit),
        cost_estimate=pl.CostEstimate(flops=flops, bytes_accessed=flops >> 9, transcendentals=0),
    )(args[0], *held)


def exchange(values, axes):
    flat = values.reshape(-1, values.shape[-1])
    return lax.all_to_all(flat, axes, 0, 0, tiled=True).reshape(values.shape)


def bands_kernel(owner_ref, *refs):
    owner, out_ref = owner_ref[0], refs[-1]
    total = refs[0][...]
    for ref in refs[1:-1]:
        total = total + ref[...]

    def tile(k):
        return total[8 * k : 8 * k + 8]

    def either(first, a, b):
        return jnp.where(owner >= first, tile(a), tile(b))

    bands = (
        [tile(k) for k in (0, 1, 2, 3, 6, 9)],
        [tile(0), either(12, 1, 7), either(12, 2, 4), either(12, 3, 5), tile(6), tile(10)],
        [tile(1), tile(2), tile(4), tile(7), either(8, 5, 8), tile(11)],
        [tile(k) for k in (2, 3, 4, 5, 8, 11)],
    )
    for k in range(16):
        for at, piece in enumerate(bands[k % 4]):
            out_ref[k, at * 8 : at * 8 + 8, :] = piece


def shards(desc, species, atom_cfg, slot, weights):
    atoms, width = desc.shape
    configs = slot.shape[0]
    cfg_here = weights.shape[0]
    n_dev = math.prod(SIZES)
    x, l, core, kind, part = [lax.axis_index(axis) for axis in AXES]
    f32 = jnp.float32

    root = jnp.broadcast_to(jnp.sqrt(weights)[:, None], (cfg_here, LANES))
    pos = jnp.stack([core, kind, part, (x * 4 + l) * 2 + core])

    flip = [(0, 1), (1, 0)]
    int_row = pltpu.VMEM((1, atoms), jnp.int32)
    matrix = pltpu.VMEM((atoms, width), jnp.bfloat16)
    sems = pltpu.SemaphoreType.DMA((6,))

    def tiles(count):
        return pltpu.VMEM((16, count * 8, LANES), f32)

    keep_s, send_s = call(
        sums_kernel,
        [tiles(12)] * 2,
        [core[None], desc, species[None], atom_cfg[None], slot[None]],
        [matrix, int_row, int_row, pltpu.VMEM((1, configs), jnp.int32), sems],
        pltpu.HBM,
        24 << 20,
        4 * configs * atoms * width,
    )
    pair_s, desc, pos, root = lax.optimization_barrier((keep_s + lax.ppermute(send_s, "c", flip), desc, pos, root))
    keep_g, *send_g = call(
        gram_kernel,
        [tiles(21)] + [tiles(6)] * 3 + [tiles(3)],
        [core[None], desc, species[None]],
        [matrix, int_row, pltpu.VMEM((width, atoms), jnp.bfloat16), sems],
        pltpu.HBM,
        24 << 20,
        4 * width * width * atoms,
    )
    pair_g = keep_g + jnp.concatenate([lax.ppermute(part_g, "c", flip) for part_g in send_g], 1)
    plane_s = jnp.sum(exchange(pair_s, ("x", "y")), 0)
    plane_s, pair_g = lax.optimization_barrier((plane_s, pair_g))
    plane_g = jnp.sum(exchange(pair_g, ("x", "y")), 0)

    def along_l(value, k):
        return lax.ppermute(value, "l", [(i, (i + k) % 4) for i in range(4)])

    plane_s = plane_s + lax.ppermute(plane_s, "h", flip)
    rooted = jnp.concatenate([plane_s, root])
    got = [(rooted, l)]
    for k in (2, 1, 3):
        got.append((along_l(rooted, k), (l - k) % 4))
    root_here = sum(jnp.where(source == part, value[96:], 0.0) for value, source in got)
    scale = 1.0 / math.sqrt(atoms * n_dev / configs)
    sums = sum(value[:96] for value, _ in got).reshape(12, 8, LANES) * (root_here * scale)
    sums, plane_g = lax.optimization_barrier((sums, plane_g))
    def of_species(which):
        return jnp.concatenate([lax.dynamic_slice_in_dim(plane_g, which * 72, 72), plane_g[144:]])

    mine_s = exchange(jnp.broadcast_to(sums.reshape(1, 96, LANES), (16, 96, LANES)), ("x", "y"))
    grams = of_species(kind) + lax.ppermute(of_species(1 - kind), "h", flip)
    (spread,) = call(
        bands_kernel,
        [tiles(6)],
        [(x * 4 + part)[None], grams] + [along_l(grams, k) for k in (2, 1, 3)],
        (),
        pltpu.VMEM,
        8 << 20,
        5500000000,
    )
    spread, mine_s = lax.optimization_barrier((spread, mine_s))
    mine_g = exchange(spread, ("x", "y"))
    band = 2 * width // 8
    norm = atoms * n_dev // 8
    cross, rows = call(
        product_kernel,
        [pltpu.VMEM((band, 2 * width), f32), jax.ShapeDtypeStruct((cfg_here, band), f32)],
        [pos, mine_s, lax.ppermute(mine_s, "c", flip), root],
        [pltpu.VMEM((configs, 2 * width), f32), pltpu.VMEM((configs, band), f32)],
        pltpu.VMEM,
        24 << 20,
        24 * band * width * configs,
    )
    mine_g, cross = lax.optimization_barrier((mine_g, cross))
    (normal,) = call(
        functools.partial(final_kernel, norm),
        [jax.ShapeDtypeStruct((band, 2 * width), f32)],
        [pos, mine_g, lax.ppermute(mine_g, "c", flip), cross],
        [pltpu.VMEM((band, width), f32)],
        pltpu.VMEM,
        24 << 20,
        band * width,
    )
    return normal, rows


def solution(mesh):
    fine = Mesh(mesh.devices.reshape(SIZES), AXES)
    return jax.shard_map(
        shards,
        mesh=fine,
        in_specs=(P(AXES, None), P(AXES), P(AXES), P(), P(("x", "l", "c"))),
        out_specs=(P(("h", "y"), None), P(("x", "l", "c"), ("h", "y"))),
        check_vma=False,
    )
```

```python
import functools
import math

import jax
import jax.numpy as jnp
from jax import lax
from jax.experimental import pallas as pl
from jax.experimental.pallas import tpu as pltpu
from jax.sharding import Mesh, PartitionSpec as P

AXES = ("x", "l", "c", "h", "y")
SIZES = (4, 4, 2, 2, 4)
TILE = 256
LANES = 128
PAIRS = ((0, 1), (0, 2), (1, 2))


def put(core, tile, index, keep_ref, send_refs, owner=0):
    tile = tile.reshape(-1, 2, 8, LANES)
    owners = slice(owner, owner + tile.shape[0])
    which, at = divmod(index * 8, send_refs[0].shape[1])
    keep_ref[owners, index * 8 : index * 8 + 8, :] = jnp.where(core == 0, tile[:, 0], tile[:, 1])
    send_refs[which][owners, at : at + 8, :] = jnp.where(core == 0, tile[:, 1], tile[:, 0])


def load(small, desc_hbm, desc_ref, sems):
    copies = [pltpu.make_async_copy(a, b, sems.at[k]) for k, (a, b) in enumerate(small)]
    for i in range(3):
        cols = slice(i * TILE, (i + 1) * TILE)
        copies.append(pltpu.make_async_copy(desc_hbm.at[:, cols], desc_ref.at[:, cols], sems.at[3 + i]))
    for copy in copies:
        copy.start()
    for copy in copies[:-3]:
        copy.wait()
    return copies[-3:]


def sums_kernel(
    core_ref,
    desc_hbm,
    species_hbm,
    cfg_hbm,
    slot_hbm,
    keep_ref,
    send_ref,
    desc_ref,
    species_ref,
    cfg_ref,
    slot_ref,
    sems,
):
    core = core_ref[0]
    atoms = desc_ref.shape[0]
    configs = slot_ref.shape[1]
    small = ((cfg_hbm, cfg_ref), (slot_hbm, slot_ref), (species_hbm, species_ref))
    blocks = load(small, desc_hbm, desc_ref, sems)
    ids = lax.broadcasted_iota(jnp.int32, (configs, atoms), 0)
    member = (cfg_ref[...] == ids).astype(jnp.bfloat16)
    rows = lax.broadcasted_iota(jnp.int32, (configs, configs), 0)
    place = (slot_ref[...] == rows).astype(jnp.bfloat16)
    placed = jnp.dot(place, member, preferred_element_type=jnp.float32).astype(jnp.bfloat16)
    members = [placed * (species_ref[...] == kind).astype(jnp.bfloat16) for kind in range(2)]
    for j in range(3):
        blocks[j].wait()
        right = desc_ref[:, j * TILE : (j + 1) * TILE]
        for kind in range(2):
            block = jnp.dot(members[kind], right, preferred_element_type=jnp.float32)
            for half in range(2):
                tile = block[:, half * LANES : (half + 1) * LANES]
                put(core, tile, kind * 6 + j * 2 + half, keep_ref, [send_ref])


def gram_kernel(core_ref, desc_hbm, species_hbm, keep_ref, *refs):
    send_refs, (desc_ref, species_ref, turned, sems) = refs[:-4], refs[-4:]
    core = core_ref[0]
    blocks = load(((species_hbm, species_ref),), desc_hbm, desc_ref, sems)
    masks = [(species_ref[...] == kind).astype(jnp.bfloat16) for kind in range(2)]
    for j in range(3):
        blocks[j].wait()
        right = desc_ref[:, j * TILE : (j + 1) * TILE]
        turned[j * TILE : (j + 1) * TILE, :] = right.T
        for i in range(j + 1):
            for kind in range(2):
                left = turned[i * TILE : (i + 1) * TILE, :] * masks[kind]
                block = jnp.dot(left, right, preferred_element_type=jnp.float32)
                if i == j:
                    put(core, block[:LANES, :LANES], 18 + i, keep_ref, send_refs, 8 * kind)
                    put(core, block[:, LANES:], kind * 9 + 6 + i, keep_ref, send_refs)
                else:
                    first = kind * 9 + PAIRS.index((i, j)) * 2
                    put(core, block[:, :LANES], first, keep_ref, send_refs)
                    put(core, block[:, LANES:], first + 1, keep_ref, send_refs)


def joined_rows(core, refs, tile, lo=0, hi=16):
    at = slice(tile * 8, (tile + 1) * 8)
    a, b = [ref[lo:hi, at, :] for ref in refs]
    pair = [jnp.where(core == which, a, b)[:, None] for which in range(2)]
    return jnp.concatenate(pair, 1).reshape((hi - lo) * 16, LANES)


def product_kernel(pos_ref, mine_ref, other_ref, root_ref, cross_ref, cfg_ref, full, left):
    core, kind, part, owner = pos_ref[0], pos_ref[1], pos_ref[2], pos_ref[3]
    width = full.shape[1] // 2
    band = left.shape[1]
    for j in range(2 * width // LANES):
        full[:, j * LANES : (j + 1) * LANES] = joined_rows(core, (mine_ref, other_ref), j)
    for k in range(4):

        @pl.when(part == k)
        def _():
            cols = slice(k * band, (k + 1) * band)
            shifted = slice(width + k * band, width + (k + 1) * band)
            left[...] = jnp.where(kind == 0, full[:, cols], full[:, shifted])
            own = pl.ds(pl.multiple_of(owner * 8, 8), 8)
            tile = jnp.where(kind == 0, full[own, cols], full[own, shifted])
            cfg_ref[...] = tile / root_ref[:, :1]

    cross = lax.dot_general(
        left[...],
        full[...],
        (((0,), (0,)), ((), ())),
        precision=lax.Precision.HIGHEST,
        preferred_element_type=jnp.float32,
    )
    cross_ref[...] = cross * (1.0 / full.shape[0])


def final_kernel(norm, pos_ref, mine_ref, other_ref, cross_ref, normal_ref, gram):
    core, kind, part = pos_ref[0], pos_ref[1], pos_ref[2]
    width = gram.shape[1]

    def joined(tile, lo=0, hi=16):
        return joined_rows(core, (mine_ref, other_ref), tile, lo, hi)

    def fill(row, col, piece):
        gram[row : row + piece.shape[0], col : col + piece.shape[1]] = piece

    def straight(tiles, lo, hi, row, col):
        for k, tile in enumerate(tiles):
            fill(row, col + k * LANES, joined(tile, lo, hi))

    def corner():
        return jnp.where(kind == 0, joined(5, 0, 8), joined(5, 8, 16))

    def band_0():
        fill(0, 0, corner())
        fill(128, 0, joined(4, 0, 8).T[:64])
        straight((4, 0, 1, 2, 3), 0, 12, 0, LANES)

    def band_1():
        fill(0, 0, joined(4, 0, 8).T[64:])
        straight((4, 0, 1, 2, 3), 12, 16, 0, LANES)
        fill(64, 0, joined(0).T)
        fill(64, TILE, corner())
        straight((1, 2, 3), 0, 8, 64, TILE + LANES)

    def band_2():
        fill(0, 0, joined(0).T)
        fill(0, TILE, joined(3, 0, 8).T)
        straight((3, 2, 4), 8, 16, 0, TILE + LANES)
        fill(128, 0, joined(1).T[:64])
        fill(128, TILE, joined(2).T[:64])
        fill(128, 2 * TILE, corner()[:64])
        straight((4,), 0, 4, 128, 2 * TILE + LANES)

    def band_3():
        fill(0, 0, joined(0).T[64:])
        fill(64, 0, joined(1).T)
        fill(0, TILE, joined(2).T[64:])
        fill(64, TILE, joined(3).T)
        fill(0, 2 * TILE, corner()[64:])
        fill(64, 2 * TILE, joined(4, 0, 8).T)
        straight((4,), 4, 16, 0, 2 * TILE + LANES)

    for k, body in enumerate((band_0, band_1, band_2, band_3)):
        pl.when(part == k)(body)

    for which in range(2):
        cols = slice(which * width, (which + 1) * width)
        extra = jnp.where(kind == which, gram[...] * (1.0 / norm), 0.0)
        normal_ref[:, cols] = cross_ref[:, cols] + extra


def call(kernel, outs, args, scratch, space, limit, flops):
    smem = pl.BlockSpec(memory_space=pltpu.SMEM)
    held = [pltpu.with_memory_space_constraint(a, space) for a in args[1:]]
    return pl.pallas_call(
        kernel,
        out_shape=outs,
        in_specs=[smem] + [pl.BlockSpec(memory_space=space)] * len(held),
        out_specs=[pl.BlockSpec(memory_space=pltpu.VMEM)] * len(outs),
        scratch_shapes=list(scratch),
        compiler_params=pltpu.CompilerParams(vmem_limit_bytes=limit),
        cost_estimate=pl.CostEstimate(flops=flops, bytes_accessed=flops >> 9, transcendentals=0),
    )(args[0], *held)


def exchange(values, axes):
    flat = values.reshape(-1, values.shape[-1])
    return lax.all_to_all(flat, axes, 0, 0, tiled=True).reshape(values.shape)


def rows_kernel(scale, from_ref, *refs):
    out_ref = refs[-1]
    total, root = 0.0, 0.0
    for k, ref in enumerate(refs[:-1]):
        total = total + ref[:96]
        root = root + jnp.where(from_ref[k] == 1, ref[96:], 0.0)
    rows = (total.reshape(12, 8, LANES) * (root * scale)).reshape(96, LANES)
    for k in range(16):
        out_ref[k] = rows


def bands_kernel(owner_ref, *refs):
    owner, out_ref = owner_ref[0], refs[-1]
    total = refs[0][...]
    for ref in refs[1:-1]:
        total = total + ref[...]

    def tile(k):
        return total[8 * k : 8 * k + 8]

    def either(first, a, b):
        return jnp.where(owner >= first, tile(a), tile(b))

    bands = (
        [tile(k) for k in (0, 1, 2, 3, 6, 9)],
        [tile(0), either(12, 1, 7), either(12, 2, 4), either(12, 3, 5), tile(6), tile(10)],
        [tile(1), tile(2), tile(4), tile(7), either(8, 5, 8), tile(11)],
        [tile(k) for k in (2, 3, 4, 5, 8, 11)],
    )
    for k in range(16):
        for at, piece in enumerate(bands[k % 4]):
            out_ref[k, at * 8 : at * 8 + 8, :] = piece


def shards(desc, species, atom_cfg, slot, weights):
    atoms, width = desc.shape
    configs = slot.shape[0]
    cfg_here = weights.shape[0]
    n_dev = math.prod(SIZES)
    x, l, core, kind, part = [lax.axis_index(axis) for axis in AXES]
    f32 = jnp.float32

    root = jnp.broadcast_to(jnp.sqrt(weights)[:, None], (cfg_here, LANES))
    pos = jnp.stack([core, kind, part, (x * 4 + l) * 2 + core])

    flip = [(0, 1), (1, 0)]
    int_row = pltpu.VMEM((1, atoms), jnp.int32)
    matrix = pltpu.VMEM((atoms, width), jnp.bfloat16)
    sems = pltpu.SemaphoreType.DMA((6,))

    def tiles(count):
        return pltpu.VMEM((16, count * 8, LANES), f32)

    keep_s, send_s = call(
        sums_kernel,
        [tiles(12)] * 2,
        [core[None], desc, species[None], atom_cfg[None], slot[None]],
        [matrix, int_row, int_row, pltpu.VMEM((1, configs), jnp.int32), sems],
        pltpu.HBM,
        24 << 20,
        4 * configs * atoms * width,
    )
    pair_s, desc, pos, root = lax.optimization_barrier((keep_s + lax.ppermute(send_s, "c", flip), desc, pos, root))
    keep_g, *send_g = call(
        gram_kernel,
        [tiles(21)] + [tiles(6)] * 3 + [tiles(3)],
        [core[None], desc, species[None]],
        [matrix, int_row, pltpu.VMEM((width, atoms), jnp.bfloat16), sems],
        pltpu.HBM,
        24 << 20,
        4 * width * width * atoms,
    )
    pair_g = keep_g + jnp.concatenate([lax.ppermute(part_g, "c", flip) for part_g in send_g], 1)
    plane_s = jnp.sum(exchange(pair_s, ("x", "y")), 0)
    plane_s, pair_g = lax.optimization_barrier((plane_s, pair_g))
    plane_g = jnp.sum(exchange(pair_g, ("x", "y")), 0)

    def along_l(value, k):
        return lax.ppermute(value, "l", [(i, (i + k) % 4) for i in range(4)])

    plane_s = plane_s + lax.ppermute(plane_s, "h", flip)
    rooted = jnp.concatenate([plane_s, root])
    got = [(rooted, l)]
    for k in (2, 1, 3):
        got.append((along_l(rooted, k), (l - k) % 4))
    scale = 1.0 / math.sqrt(atoms * n_dev / configs)
    (sums,) = call(
        functools.partial(rows_kernel, scale),
        [tiles(12)],
        [jnp.stack([source == part for _, source in got]).astype(jnp.int32)] + [value for value, _ in got],
        (),
        pltpu.VMEM,
        8 << 20,
        1 << 20,
    )
    sums, plane_g = lax.optimization_barrier((sums, plane_g))
    def of_species(which):
        return jnp.concatenate([lax.dynamic_slice_in_dim(plane_g, which * 72, 72), plane_g[144:]])

    mine_s = exchange(sums, ("x", "y"))
    grams = of_species(kind) + lax.ppermute(of_species(1 - kind), "h", flip)
    (spread,) = call(
        bands_kernel,
        [tiles(6)],
        [(x * 4 + part)[None], grams] + [along_l(grams, k) for k in (2, 1, 3)],
        (),
        pltpu.VMEM,
        8 << 20,
        5500000000,
    )
    spread, mine_s = lax.optimization_barrier((spread, mine_s))
    mine_g = exchange(spread, ("x", "y"))
    band = 2 * width // 8
    norm = atoms * n_dev // 8
    cross, rows = call(
        product_kernel,
        [pltpu.VMEM((band, 2 * width), f32), jax.ShapeDtypeStruct((cfg_here, band), f32)],
        [pos, mine_s, lax.ppermute(mine_s, "c", flip), root],
        [pltpu.VMEM((configs, 2 * width), f32), pltpu.VMEM((configs, band), f32)],
        pltpu.VMEM,
        24 << 20,
        24 * band * width * configs,
    )
    mine_g, cross = lax.optimization_barrier((mine_g, cross))
    (normal,) = call(
        functools.partial(final_kernel, norm),
        [jax.ShapeDtypeStruct((band, 2 * width), f32)],
        [pos, mine_g, lax.ppermute(mine_g, "c", flip), cross],
        [pltpu.VMEM((band, width), f32)],
        pltpu.VMEM,
        24 << 20,
        band * width,
    )
    return normal, rows


def solution(mesh):
    fine = Mesh(mesh.devices.reshape(SIZES), AXES)
    return jax.shard_map(
        shards,
        mesh=fine,
        in_specs=(P(AXES, None), P(AXES), P(AXES), P(), P(("x", "l", "c"))),
        out_specs=(P(("h", "y"), None), P(("x", "l", "c"), ("h", "y"))),
        check_vma=False,
    )
```

```python
import functools
import math

import jax
import jax.numpy as jnp
from jax import lax
from jax.experimental import pallas as pl
from jax.experimental.pallas import tpu as pltpu
from jax.sharding import Mesh, PartitionSpec as P

AXES = ("x", "l", "c", "h", "y")
SIZES = (4, 4, 2, 2, 4)
TILE = 256
LANES = 128
PAIRS = ((0, 1), (0, 2), (1, 2))


def put(core, tile, index, keep_ref, send_refs, owner=0):
    tile = tile.reshape(-1, 2, 8, LANES)
    owners = slice(owner, owner + tile.shape[0])
    which, at = divmod(index * 8, send_refs[0].shape[1])
    keep_ref[owners, index * 8 : index * 8 + 8, :] = jnp.where(core == 0, tile[:, 0], tile[:, 1])
    send_refs[which][owners, at : at + 8, :] = jnp.where(core == 0, tile[:, 1], tile[:, 0])


def load(small, desc_hbm, desc_ref, sems):
    copies = [pltpu.make_async_copy(a, b, sems.at[k]) for k, (a, b) in enumerate(small)]
    for i in range(3):
        cols = slice(i * TILE, (i + 1) * TILE)
        copies.append(pltpu.make_async_copy(desc_hbm.at[:, cols], desc_ref.at[:, cols], sems.at[3 + i]))
    for copy in copies:
        copy.start()
    for copy in copies[:-3]:
        copy.wait()
    return copies[-3:]


def sums_kernel(
    core_ref,
    desc_hbm,
    species_hbm,
    cfg_hbm,
    slot_hbm,
    keep_ref,
    send_ref,
    desc_ref,
    species_ref,
    cfg_ref,
    slot_ref,
    sems,
):
    core = core_ref[0]
    atoms = desc_ref.shape[0]
    configs = slot_ref.shape[1]
    small = ((cfg_hbm, cfg_ref), (slot_hbm, slot_ref), (species_hbm, species_ref))
    blocks = load(small, desc_hbm, desc_ref, sems)
    ids = lax.broadcasted_iota(jnp.int32, (configs, atoms), 0)
    member = (cfg_ref[...] == ids).astype(jnp.bfloat16)
    rows = lax.broadcasted_iota(jnp.int32, (configs, configs), 0)
    place = (slot_ref[...] == rows).astype(jnp.bfloat16)
    placed = jnp.dot(place, member, preferred_element_type=jnp.float32).astype(jnp.bfloat16)
    members = [placed * (species_ref[...] == kind).astype(jnp.bfloat16) for kind in range(2)]
    for j in range(3):
        blocks[j].wait()
        right = desc_ref[:, j * TILE : (j + 1) * TILE]
        for kind in range(2):
            block = jnp.dot(members[kind], right, preferred_element_type=jnp.float32)
            for half in range(2):
                tile = block[:, half * LANES : (half + 1) * LANES]
                put(core, tile, kind * 6 + j * 2 + half, keep_ref, [send_ref])


def gram_kernel(core_ref, desc_hbm, species_hbm, keep_ref, *refs):
    send_refs, (desc_ref, species_ref, turned, sems) = refs[:-4], refs[-4:]
    core = core_ref[0]
    blocks = load(((species_hbm, species_ref),), desc_hbm, desc_ref, sems)
    masks = [(species_ref[...] == kind).astype(jnp.bfloat16) for kind in range(2)]
    for j in range(3):
        blocks[j].wait()
        right = desc_ref[:, j * TILE : (j + 1) * TILE]
        turned[j * TILE : (j + 1) * TILE, :] = right.T
        for i in range(j + 1):
            for kind in range(2):
                left = turned[i * TILE : (i + 1) * TILE, :] * masks[kind]
                block = jnp.dot(left, right, preferred_element_type=jnp.float32)
                if i == j:
                    put(core, block[:LANES, :LANES], 18 + i, keep_ref, send_refs, 8 * kind)
                    put(core, block[:, LANES:], kind * 9 + 6 + i, keep_ref, send_refs)
                else:
                    first = kind * 9 + PAIRS.index((i, j)) * 2
                    put(core, block[:, :LANES], first, keep_ref, send_refs)
                    put(core, block[:, LANES:], first + 1, keep_ref, send_refs)


def joined_rows(core, refs, tile, lo=0, hi=16):
    at = slice(tile * 8, (tile + 1) * 8)
    a, b = [ref[lo:hi, at, :] for ref in refs]
    pair = [jnp.where(core == which, a, b)[:, None] for which in range(2)]
    return jnp.concatenate(pair, 1).reshape((hi - lo) * 16, LANES)


def product_kernel(pos_ref, mine_ref, *refs):
    other_refs, (root_ref, cross_ref, cfg_ref, full, left) = refs[:-5], refs[-5:]
    core, kind, part, owner = pos_ref[0], pos_ref[1], pos_ref[2], pos_ref[3]
    width = full.shape[1] // 2
    band = left.shape[1]
    owners = other_refs[0].shape[0]
    for k, other_ref in enumerate(other_refs):
        for j in range(2 * width // LANES):
            part_refs = (mine_ref.at[k * owners : (k + 1) * owners], other_ref)
            piece = joined_rows(core, part_refs, j, 0, owners)
            full[k * owners * 16 : (k + 1) * owners * 16, j * LANES : (j + 1) * LANES] = piece
    for k in range(4):

        @pl.when(part == k)
        def _():
            cols = slice(k * band, (k + 1) * band)
            shifted = slice(width + k * band, width + (k + 1) * band)
            left[...] = jnp.where(kind == 0, full[:, cols], full[:, shifted])
            own = pl.ds(pl.multiple_of(owner * 8, 8), 8)
            tile = jnp.where(kind == 0, full[own, cols], full[own, shifted])
            cfg_ref[...] = tile / root_ref[:, :1]

    cross = lax.dot_general(
        left[...],
        full[...],
        (((0,), (0,)), ((), ())),
        precision=lax.Precision.HIGHEST,
        preferred_element_type=jnp.float32,
    )
    cross_ref[...] = cross * (1.0 / full.shape[0])


def final_kernel(norm, pos_ref, mine_ref, other_ref, cross_ref, normal_ref, gram):
    core, kind, part = pos_ref[0], pos_ref[1], pos_ref[2]
    width = gram.shape[1]

    def joined(tile, lo=0, hi=16):
        return joined_rows(core, (mine_ref, other_ref), tile, lo, hi)

    def fill(row, col, piece):
        gram[row : row + piece.shape[0], col : col + piece.shape[1]] = piece

    def straight(tiles, lo, hi, row, col):
        for k, tile in enumerate(tiles):
            fill(row, col + k * LANES, joined(tile, lo, hi))

    def corner():
        return jnp.where(kind == 0, joined(5, 0, 8), joined(5, 8, 16))

    def band_0():
        fill(0, 0, corner())
        fill(128, 0, joined(4, 0, 8).T[:64])
        straight((4, 0, 1, 2, 3), 0, 12, 0, LANES)

    def band_1():
        fill(0, 0, joined(4, 0, 8).T[64:])
        straight((4, 0, 1, 2, 3), 12, 16, 0, LANES)
        fill(64, 0, joined(0).T)
        fill(64, TILE, corner())
        straight((1, 2, 3), 0, 8, 64, TILE + LANES)

    def band_2():
        fill(0, 0, joined(0).T)
        fill(0, TILE, joined(3, 0, 8).T)
        straight((3, 2, 4), 8, 16, 0, TILE + LANES)
        fill(128, 0, joined(1).T[:64])
        fill(128, TILE, joined(2).T[:64])
        fill(128, 2 * TILE, corner()[:64])
        straight((4,), 0, 4, 128, 2 * TILE + LANES)

    def band_3():
        fill(0, 0, joined(0).T[64:])
        fill(64, 0, joined(1).T)
        fill(0, TILE, joined(2).T[64:])
        fill(64, TILE, joined(3).T)
        fill(0, 2 * TILE, corner()[64:])
        fill(64, 2 * TILE, joined(4, 0, 8).T)
        straight((4,), 4, 16, 0, 2 * TILE + LANES)

    for k, body in enumerate((band_0, band_1, band_2, band_3)):
        pl.when(part == k)(body)

    for which in range(2):
        cols = slice(which * width, (which + 1) * width)
        extra = jnp.where(kind == which, gram[...] * (1.0 / norm), 0.0)
        normal_ref[:, cols] = cross_ref[:, cols] + extra


def call(kernel, outs, args, scratch, space, limit, flops):
    smem = pl.BlockSpec(memory_space=pltpu.SMEM)
    held = [pltpu.with_memory_space_constraint(a, space) for a in args[1:]]
    return pl.pallas_call(
        kernel,
        out_shape=outs,
        in_specs=[smem] + [pl.BlockSpec(memory_space=space)] * len(held),
        out_specs=[pl.BlockSpec(memory_space=pltpu.VMEM)] * len(outs),
        scratch_shapes=list(scratch),
        compiler_params=pltpu.CompilerParams(vmem_limit_bytes=limit),
        cost_estimate=pl.CostEstimate(flops=flops, bytes_accessed=flops >> 9, transcendentals=0),
    )(args[0], *held)


def exchange(values, axes):
    flat = values.reshape(-1, values.shape[-1])
    return lax.all_to_all(flat, axes, 0, 0, tiled=True).reshape(values.shape)


def bands_kernel(owner_ref, *refs):
    owner, out_ref = owner_ref[0], refs[-1]
    total = refs[0][...]
    for ref in refs[1:-1]:
        total = total + ref[...]

    def tile(k):
        return total[8 * k : 8 * k + 8]

    def either(first, a, b):
        return jnp.where(owner >= first, tile(a), tile(b))

    bands = (
        [tile(k) for k in (0, 1, 2, 3, 6, 9)],
        [tile(0), either(12, 1, 7), either(12, 2, 4), either(12, 3, 5), tile(6), tile(10)],
        [tile(1), tile(2), tile(4), tile(7), either(8, 5, 8), tile(11)],
        [tile(k) for k in (2, 3, 4, 5, 8, 11)],
    )
    for k in range(16):
        for at, piece in enumerate(bands[k % 4]):
            out_ref[k, at * 8 : at * 8 + 8, :] = piece


def shards(desc, species, atom_cfg, slot, weights):
    atoms, width = desc.shape
    configs = slot.shape[0]
    cfg_here = weights.shape[0]
    n_dev = math.prod(SIZES)
    x, l, core, kind, part = [lax.axis_index(axis) for axis in AXES]
    f32 = jnp.float32

    root = jnp.broadcast_to(jnp.sqrt(weights)[:, None], (cfg_here, LANES))
    pos = jnp.stack([core, kind, part, (x * 4 + l) * 2 + core])

    flip = [(0, 1), (1, 0)]
    int_row = pltpu.VMEM((1, atoms), jnp.int32)
    matrix = pltpu.VMEM((atoms, width), jnp.bfloat16)
    sems = pltpu.SemaphoreType.DMA((6,))

    def tiles(count):
        return pltpu.VMEM((16, count * 8, LANES), f32)

    keep_s, send_s = call(
        sums_kernel,
        [tiles(12)] * 2,
        [core[None], desc, species[None], atom_cfg[None], slot[None]],
        [matrix, int_row, int_row, pltpu.VMEM((1, configs), jnp.int32), sems],
        pltpu.HBM,
        24 << 20,
        4 * configs * atoms * width,
    )
    pair_s, desc, pos, root = lax.optimization_barrier((keep_s + lax.ppermute(send_s, "c", flip), desc, pos, root))
    keep_g, *send_g = call(
        gram_kernel,
        [tiles(21)] + [tiles(6)] * 3 + [tiles(3)],
        [core[None], desc, species[None]],
        [matrix, int_row, pltpu.VMEM((width, atoms), jnp.bfloat16), sems],
        pltpu.HBM,
        24 << 20,
        4 * width * width * atoms,
    )
    pair_g = keep_g + jnp.concatenate([lax.ppermute(part_g, "c", flip) for part_g in send_g], 1)
    plane_s = jnp.sum(exchange(pair_s, ("x", "y")), 0)
    plane_s, pair_g = lax.optimization_barrier((plane_s, pair_g))
    plane_g = jnp.sum(exchange(pair_g, ("x", "y")), 0)

    def along_l(value, k):
        return lax.ppermute(value, "l", [(i, (i + k) % 4) for i in range(4)])

    plane_s = plane_s + lax.ppermute(plane_s, "h", flip)
    rooted = jnp.concatenate([plane_s, root])
    got = [(rooted, l)]
    for k in (2, 1, 3):
        got.append((along_l(rooted, k), (l - k) % 4))
    root_here = sum(jnp.where(source == part, value[96:], 0.0) for value, source in got)
    scale = 1.0 / math.sqrt(atoms * n_dev / configs)
    sums = sum(value[:96] for value, _ in got).reshape(12, 8, LANES) * (root_here * scale)
    sums, plane_g = lax.optimization_barrier((sums, plane_g))
    def of_species(which):
        return jnp.concatenate([lax.dynamic_slice_in_dim(plane_g, which * 72, 72), plane_g[144:]])

    mine_s = exchange(jnp.broadcast_to(sums.reshape(1, 96, LANES), (16, 96, LANES)), ("x", "y"))
    grams = of_species(kind) + lax.ppermute(of_species(1 - kind), "h", flip)
    (spread,) = call(
        bands_kernel,
        [tiles(6)],
        [(x * 4 + part)[None], grams] + [along_l(grams, k) for k in (2, 1, 3)],
        (),
        pltpu.VMEM,
        8 << 20,
        5500000000,
    )
    spread, mine_s = lax.optimization_barrier((spread, mine_s))
    mine_g = exchange(spread, ("x", "y"))
    band = 2 * width // 8
    norm = atoms * n_dev // 8
    cross, rows = call(
        product_kernel,
        [pltpu.VMEM((band, 2 * width), f32), jax.ShapeDtypeStruct((cfg_here, band), f32)],
        [pos, mine_s] + [lax.ppermute(mine_s[k : k + 4], "c", flip) for k in range(0, 16, 4)] + [root],
        [pltpu.VMEM((configs, 2 * width), f32), pltpu.VMEM((configs, band), f32)],
        pltpu.VMEM,
        24 << 20,
        24 * band * width * configs,
    )
    mine_g, cross = lax.optimization_barrier((mine_g, cross))
    (normal,) = call(
        functools.partial(final_kernel, norm),
        [jax.ShapeDtypeStruct((band, 2 * width), f32)],
        [pos, mine_g, lax.ppermute(mine_g, "c", flip), cross],
        [pltpu.VMEM((band, width), f32)],
        pltpu.VMEM,
        24 << 20,
        band * width,
    )
    return normal, rows


def solution(mesh):
    fine = Mesh(mesh.devices.reshape(SIZES), AXES)
    return jax.shard_map(
        shards,
        mesh=fine,
        in_specs=(P(AXES, None), P(AXES), P(AXES), P(), P(("x", "l", "c"))),
        out_specs=(P(("h", "y"), None), P(("x", "l", "c"), ("h", "y"))),
        check_vma=False,
    )
```

```python
import functools
import math

import jax
import jax.numpy as jnp
from jax import lax
from jax.experimental import pallas as pl
from jax.experimental.pallas import tpu as pltpu
from jax.sharding import Mesh, PartitionSpec as P

AXES = ("x", "l", "c", "h", "y")
SIZES = (4, 4, 2, 2, 4)
TILE = 256
LANES = 128
PAIRS = ((0, 1), (0, 2), (1, 2))


def put(core, tile, index, keep_ref, send_refs, owner=0):
    tile = tile.reshape(-1, 2, 8, LANES)
    owners = slice(owner, owner + tile.shape[0])
    which, at = divmod(index * 8, send_refs[0].shape[1])
    keep_ref[owners, index * 8 : index * 8 + 8, :] = jnp.where(core == 0, tile[:, 0], tile[:, 1])
    send_refs[which][owners, at : at + 8, :] = jnp.where(core == 0, tile[:, 1], tile[:, 0])


def load(small, desc_hbm, desc_ref, sems):
    copies = [pltpu.make_async_copy(a, b, sems.at[k]) for k, (a, b) in enumerate(small)]
    for i in range(3):
        cols = slice(i * TILE, (i + 1) * TILE)
        copies.append(pltpu.make_async_copy(desc_hbm.at[:, cols], desc_ref.at[:, cols], sems.at[3 + i]))
    for copy in copies:
        copy.start()
    for copy in copies[:-3]:
        copy.wait()
    return copies[-3:]


def sums_kernel(
    core_ref,
    desc_hbm,
    species_hbm,
    cfg_hbm,
    slot_hbm,
    keep_ref,
    send_ref,
    desc_ref,
    species_ref,
    cfg_ref,
    slot_ref,
    sems,
):
    core = core_ref[0]
    atoms = desc_ref.shape[0]
    configs = slot_ref.shape[1]
    small = ((cfg_hbm, cfg_ref), (slot_hbm, slot_ref), (species_hbm, species_ref))
    blocks = load(small, desc_hbm, desc_ref, sems)
    ids = lax.broadcasted_iota(jnp.int32, (configs, atoms), 0)
    member = (cfg_ref[...] == ids).astype(jnp.bfloat16)
    rows = lax.broadcasted_iota(jnp.int32, (configs, configs), 0)
    place = (slot_ref[...] == rows).astype(jnp.bfloat16)
    placed = jnp.dot(place, member, preferred_element_type=jnp.float32).astype(jnp.bfloat16)
    members = [placed * (species_ref[...] == kind).astype(jnp.bfloat16) for kind in range(2)]
    for j in range(3):
        blocks[j].wait()
        right = desc_ref[:, j * TILE : (j + 1) * TILE]
        for kind in range(2):
            block = jnp.dot(members[kind], right, preferred_element_type=jnp.float32)
            for half in range(2):
                tile = block[:, half * LANES : (half + 1) * LANES]
                put(core, tile, kind * 6 + j * 2 + half, keep_ref, [send_ref])


def gram_kernel(core_ref, desc_hbm, species_hbm, keep_ref, *refs):
    send_refs, (desc_ref, species_ref, turned, sems) = refs[:-4], refs[-4:]
    core = core_ref[0]
    blocks = load(((species_hbm, species_ref),), desc_hbm, desc_ref, sems)
    masks = [(species_ref[...] == kind).astype(jnp.bfloat16) for kind in range(2)]
    for j in range(3):
        blocks[j].wait()
        right = desc_ref[:, j * TILE : (j + 1) * TILE]
        turned[j * TILE : (j + 1) * TILE, :] = right.T
        for i in range(j + 1):
            for kind in range(2):
                left = turned[i * TILE : (i + 1) * TILE, :] * masks[kind]
                block = jnp.dot(left, right, preferred_element_type=jnp.float32)
                if i == j:
                    put(core, block[:LANES, :LANES], 18 + i, keep_ref, send_refs, 8 * kind)
                    put(core, block[:, LANES:], kind * 9 + 6 + i, keep_ref, send_refs)
                else:
                    first = kind * 9 + PAIRS.index((i, j)) * 2
                    put(core, block[:, :LANES], first, keep_ref, send_refs)
                    put(core, block[:, LANES:], first + 1, keep_ref, send_refs)


def joined_rows(core, refs, tile, lo=0, hi=16):
    at = slice(tile * 8, (tile + 1) * 8)
    a, b = [ref[lo:hi, at, :] for ref in refs]
    pair = [jnp.where(core == which, a, b)[:, None] for which in range(2)]
    return jnp.concatenate(pair, 1).reshape((hi - lo) * 16, LANES)


def product_kernel(pos_ref, mine_ref, *refs):
    other_refs, (root_ref, cross_ref, cfg_ref, full, left) = refs[:-5], refs[-5:]
    core, kind, part, owner = pos_ref[0], pos_ref[1], pos_ref[2], pos_ref[3]
    width = full.shape[1] // 2
    band = left.shape[1]
    owners = other_refs[0].shape[0]
    for k, other_ref in enumerate(other_refs):
        for j in range(2 * width // LANES):
            part_refs = (mine_ref.at[k * owners : (k + 1) * owners], other_ref)
            piece = joined_rows(core, part_refs, j, 0, owners)
            full[k * owners * 16 : (k + 1) * owners * 16, j * LANES : (j + 1) * LANES] = piece
    for k in range(4):

        @pl.when(part == k)
        def _():
            cols = slice(k * band, (k + 1) * band)
            shifted = slice(width + k * band, width + (k + 1) * band)
            left[...] = jnp.where(kind == 0, full[:, cols], full[:, shifted])
            own = pl.ds(pl.multiple_of(owner * 8, 8), 8)
            tile = jnp.where(kind == 0, full[own, cols], full[own, shifted])
            cfg_ref[...] = tile / root_ref[:, :1]

    cross = lax.dot_general(
        left[...],
        full[...],
        (((0,), (0,)), ((), ())),
        precision=lax.Precision.HIGHEST,
        preferred_element_type=jnp.float32,
    )
    cross_ref[...] = cross * (1.0 / full.shape[0])


def final_kernel(norm, pos_ref, mine_ref, other_ref, cross_ref, normal_ref, gram):
    core, kind, part = pos_ref[0], pos_ref[1], pos_ref[2]
    width = gram.shape[1]

    def joined(tile, lo=0, hi=16):
        return joined_rows(core, (mine_ref, other_ref), tile, lo, hi)

    def fill(row, col, piece):
        gram[row : row + piece.shape[0], col : col + piece.shape[1]] = piece

    def straight(tiles, lo, hi, row, col):
        for k, tile in enumerate(tiles):
            fill(row, col + k * LANES, joined(tile, lo, hi))

    def corner():
        return jnp.where(kind == 0, joined(5, 0, 8), joined(5, 8, 16))

    def band_0():
        fill(0, 0, corner())
        fill(128, 0, joined(4, 0, 8).T[:64])
        straight((4, 0, 1, 2, 3), 0, 12, 0, LANES)

    def band_1():
        fill(0, 0, joined(4, 0, 8).T[64:])
        straight((4, 0, 1, 2, 3), 12, 16, 0, LANES)
        fill(64, 0, joined(0).T)
        fill(64, TILE, corner())
        straight((1, 2, 3), 0, 8, 64, TILE + LANES)

    def band_2():
        fill(0, 0, joined(0).T)
        fill(0, TILE, joined(3, 0, 8).T)
        straight((3, 2, 4), 8, 16, 0, TILE + LANES)
        fill(128, 0, joined(1).T[:64])
        fill(128, TILE, joined(2).T[:64])
        fill(128, 2 * TILE, corner()[:64])
        straight((4,), 0, 4, 128, 2 * TILE + LANES)

    def band_3():
        fill(0, 0, joined(0).T[64:])
        fill(64, 0, joined(1).T)
        fill(0, TILE, joined(2).T[64:])
        fill(64, TILE, joined(3).T)
        fill(0, 2 * TILE, corner()[64:])
        fill(64, 2 * TILE, joined(4, 0, 8).T)
        straight((4,), 4, 16, 0, 2 * TILE + LANES)

    for k, body in enumerate((band_0, band_1, band_2, band_3)):
        pl.when(part == k)(body)

    for which in range(2):
        cols = slice(which * width, (which + 1) * width)
        extra = jnp.where(kind == which, gram[...] * (1.0 / norm), 0.0)
        normal_ref[:, cols] = cross_ref[:, cols] + extra


def call(kernel, outs, args, scratch, space, limit, flops):
    smem = pl.BlockSpec(memory_space=pltpu.SMEM)
    held = [pltpu.with_memory_space_constraint(a, space) for a in args[1:]]
    return pl.pallas_call(
        kernel,
        out_shape=outs,
        in_specs=[smem] + [pl.BlockSpec(memory_space=space)] * len(held),
        out_specs=[pl.BlockSpec(memory_space=pltpu.VMEM)] * len(outs),
        scratch_shapes=list(scratch),
        compiler_params=pltpu.CompilerParams(vmem_limit_bytes=limit),
        cost_estimate=pl.CostEstimate(flops=flops, bytes_accessed=flops >> 9, transcendentals=0),
    )(args[0], *held)


def exchange(values, axes):
    flat = values.reshape(-1, values.shape[-1])
    return lax.all_to_all(flat, axes, 0, 0, tiled=True).reshape(values.shape)


def rows_kernel(scale, from_ref, *refs):
    out_ref = refs[-1]
    total, root = 0.0, 0.0
    for k, ref in enumerate(refs[:-1]):
        total = total + ref[:96]
        root = root + jnp.where(from_ref[k] == 1, ref[96:], 0.0)
    rows = (total.reshape(12, 8, LANES) * (root * scale)).reshape(96, LANES)
    for k in range(16):
        out_ref[k] = rows


def bands_kernel(owner_ref, *refs):
    owner, out_ref = owner_ref[0], refs[-1]
    total = refs[0][...]
    for ref in refs[1:-1]:
        total = total + ref[...]

    def tile(k):
        return total[8 * k : 8 * k + 8]

    def either(first, a, b):
        return jnp.where(owner >= first, tile(a), tile(b))

    bands = (
        [tile(k) for k in (0, 1, 2, 3, 6, 9)],
        [tile(0), either(12, 1, 7), either(12, 2, 4), either(12, 3, 5), tile(6), tile(10)],
        [tile(1), tile(2), tile(4), tile(7), either(8, 5, 8), tile(11)],
        [tile(k) for k in (2, 3, 4, 5, 8, 11)],
    )
    for k in range(16):
        for at, piece in enumerate(bands[k % 4]):
            out_ref[k, at * 8 : at * 8 + 8, :] = piece


def shards(desc, species, atom_cfg, slot, weights):
    atoms, width = desc.shape
    configs = slot.shape[0]
    cfg_here = weights.shape[0]
    n_dev = math.prod(SIZES)
    x, l, core, kind, part = [lax.axis_index(axis) for axis in AXES]
    f32 = jnp.float32

    root = jnp.broadcast_to(jnp.sqrt(weights)[:, None], (cfg_here, LANES))
    pos = jnp.stack([core, kind, part, (x * 4 + l) * 2 + core])

    flip = [(0, 1), (1, 0)]
    int_row = pltpu.VMEM((1, atoms), jnp.int32)
    matrix = pltpu.VMEM((atoms, width), jnp.bfloat16)
    sems = pltpu.SemaphoreType.DMA((6,))

    def tiles(count):
        return pltpu.VMEM((16, count * 8, LANES), f32)

    keep_s, send_s = call(
        sums_kernel,
        [tiles(12)] * 2,
        [core[None], desc, species[None], atom_cfg[None], slot[None]],
        [matrix, int_row, int_row, pltpu.VMEM((1, configs), jnp.int32), sems],
        pltpu.HBM,
        24 << 20,
        4 * configs * atoms * width,
    )
    pair_s, desc, pos, root = lax.optimization_barrier((keep_s + lax.ppermute(send_s, "c", flip), desc, pos, root))
    keep_g, *send_g = call(
        gram_kernel,
        [tiles(21)] + [tiles(6)] * 3 + [tiles(3)],
        [core[None], desc, species[None]],
        [matrix, int_row, pltpu.VMEM((width, atoms), jnp.bfloat16), sems],
        pltpu.HBM,
        24 << 20,
        4 * width * width * atoms,
    )
    pair_g = keep_g + jnp.concatenate([lax.ppermute(part_g, "c", flip) for part_g in send_g], 1)
    plane_s = jnp.sum(exchange(pair_s, ("x", "y")), 0)
    plane_s, pair_g = lax.optimization_barrier((plane_s, pair_g))
    plane_g = jnp.sum(exchange(pair_g, ("x", "y")), 0)

    def along_l(value, k):
        return lax.ppermute(value, "l", [(i, (i + k) % 4) for i in range(4)])

    plane_s = plane_s + lax.ppermute(plane_s, "h", flip)
    rooted = jnp.concatenate([plane_s, root])
    got = [(rooted, l)]
    for k in (2, 1, 3):
        got.append((along_l(rooted, k), (l - k) % 4))
    scale = 1.0 / math.sqrt(atoms * n_dev / configs)
    (sums,) = call(
        functools.partial(rows_kernel, scale),
        [tiles(12)],
        [jnp.stack([source == part for _, source in got]).astype(jnp.int32)] + [value for value, _ in got],
        (),
        pltpu.VMEM,
        8 << 20,
        1 << 20,
    )
    sums, plane_g = lax.optimization_barrier((sums, plane_g))
    def of_species(which):
        return jnp.concatenate([lax.dynamic_slice_in_dim(plane_g, which * 72, 72), plane_g[144:]])

    mine_s = exchange(sums, ("x", "y"))
    grams = of_species(kind) + lax.ppermute(of_species(1 - kind), "h", flip)
    (spread,) = call(
        bands_kernel,
        [tiles(6)],
        [(x * 4 + part)[None], grams] + [along_l(grams, k) for k in (2, 1, 3)],
        (),
        pltpu.VMEM,
        8 << 20,
        5500000000,
    )
    spread, mine_s = lax.optimization_barrier((spread, mine_s))
    mine_g = exchange(spread, ("x", "y"))
    band = 2 * width // 8
    norm = atoms * n_dev // 8
    cross, rows = call(
        product_kernel,
        [pltpu.VMEM((band, 2 * width), f32), jax.ShapeDtypeStruct((cfg_here, band), f32)],
        [pos, mine_s] + [lax.ppermute(mine_s[k : k + 4], "c", flip) for k in range(0, 16, 4)] + [root],
        [pltpu.VMEM((configs, 2 * width), f32), pltpu.VMEM((configs, band), f32)],
        pltpu.VMEM,
        24 << 20,
        24 * band * width * configs,
    )
    mine_g, cross = lax.optimization_barrier((mine_g, cross))
    (normal,) = call(
        functools.partial(final_kernel, norm),
        [jax.ShapeDtypeStruct((band, 2 * width), f32)],
        [pos, mine_g, lax.ppermute(mine_g, "c", flip), cross],
        [pltpu.VMEM((band, width), f32)],
        pltpu.VMEM,
        24 << 20,
        band * width,
    )
    return normal, rows


def solution(mesh):
    fine = Mesh(mesh.devices.reshape(SIZES), AXES)
    return jax.shard_map(
        shards,
        mesh=fine,
        in_specs=(P(AXES, None), P(AXES), P(AXES), P(), P(("x", "l", "c"))),
        out_specs=(P(("h", "y"), None), P(("x", "l", "c"), ("h", "y"))),
        check_vma=False,
    )
```

```python
import functools
import math

import jax
import jax.numpy as jnp
from jax import lax
from jax.experimental import pallas as pl
from jax.experimental.pallas import tpu as pltpu
from jax.sharding import Mesh, PartitionSpec as P

AXES = ("x", "l", "c", "h", "y")
SIZES = (4, 4, 2, 2, 4)
TILE = 256
LANES = 128
PAIRS = ((0, 1), (0, 2), (1, 2))


def put(core, tile, index, keep_ref, send_refs, owner=0):
    tile = tile.reshape(-1, 2, 8, LANES)
    owners = slice(owner, owner + tile.shape[0])
    which, at = divmod(index * 8, send_refs[0].shape[1])
    keep_ref[owners, index * 8 : index * 8 + 8, :] = jnp.where(core == 0, tile[:, 0], tile[:, 1])
    send_refs[which][owners, at : at + 8, :] = jnp.where(core == 0, tile[:, 1], tile[:, 0])


def load(small, desc_hbm, desc_ref, sems):
    copies = [pltpu.make_async_copy(a, b, sems.at[k]) for k, (a, b) in enumerate(small)]
    for i in range(3):
        cols = slice(i * TILE, (i + 1) * TILE)
        copies.append(pltpu.make_async_copy(desc_hbm.at[:, cols], desc_ref.at[:, cols], sems.at[3 + i]))
    for copy in copies:
        copy.start()
    for copy in copies[:-3]:
        copy.wait()
    return copies[-3:]


def sums_kernel(
    core_ref,
    desc_hbm,
    species_hbm,
    cfg_hbm,
    slot_hbm,
    keep_ref,
    send_ref,
    desc_ref,
    species_ref,
    cfg_ref,
    slot_ref,
    sems,
):
    core = core_ref[0]
    atoms = desc_ref.shape[0]
    configs = slot_ref.shape[1]
    small = ((cfg_hbm, cfg_ref), (slot_hbm, slot_ref), (species_hbm, species_ref))
    blocks = load(small, desc_hbm, desc_ref, sems)
    ids = lax.broadcasted_iota(jnp.int32, (configs, atoms), 0)
    member = (cfg_ref[...] == ids).astype(jnp.bfloat16)
    rows = lax.broadcasted_iota(jnp.int32, (configs, configs), 0)
    place = (slot_ref[...] == rows).astype(jnp.bfloat16)
    placed = jnp.dot(place, member, preferred_element_type=jnp.float32).astype(jnp.bfloat16)
    members = [placed * (species_ref[...] == kind).astype(jnp.bfloat16) for kind in range(2)]
    for j in range(3):
        blocks[j].wait()
        right = desc_ref[:, j * TILE : (j + 1) * TILE]
        for kind in range(2):
            block = jnp.dot(members[kind], right, preferred_element_type=jnp.float32)
            for half in range(2):
                tile = block[:, half * LANES : (half + 1) * LANES]
                put(core, tile, kind * 6 + j * 2 + half, keep_ref, [send_ref])


def gram_kernel(core_ref, desc_hbm, species_hbm, keep_ref, *refs):
    send_refs, (desc_ref, species_ref, turned, sems) = refs[:-4], refs[-4:]
    core = core_ref[0]
    blocks = load(((species_hbm, species_ref),), desc_hbm, desc_ref, sems)
    masks = [(species_ref[...] == kind).astype(jnp.bfloat16) for kind in range(2)]
    for j in range(3):
        blocks[j].wait()
        right = desc_ref[:, j * TILE : (j + 1) * TILE]
        turned[j * TILE : (j + 1) * TILE, :] = right.T
        for i in range(j + 1):
            for kind in range(2):
                left = turned[i * TILE : (i + 1) * TILE, :] * masks[kind]
                block = jnp.dot(left, right, preferred_element_type=jnp.float32)
                if i == j:
                    put(core, block[:LANES, :LANES], 18 + i, keep_ref, send_refs, 8 * kind)
                    put(core, block[:, LANES:], kind * 9 + 6 + i, keep_ref, send_refs)
                else:
                    first = kind * 9 + PAIRS.index((i, j)) * 2
                    put(core, block[:, :LANES], first, keep_ref, send_refs)
                    put(core, block[:, LANES:], first + 1, keep_ref, send_refs)


def joined_rows(core, refs, tile, lo=0, hi=16):
    at = slice(tile * 8, (tile + 1) * 8)
    a, b = [ref[lo:hi, at, :] for ref in refs]
    pair = [jnp.where(core == which, a, b)[:, None] for which in range(2)]
    return jnp.concatenate(pair, 1).reshape((hi - lo) * 16, LANES)


def product_kernel(pos_ref, mine_ref, *refs):
    other_refs, (root_ref, cross_ref, cfg_ref, full, left) = refs[:-5], refs[-5:]
    core, kind, part, owner = pos_ref[0], pos_ref[1], pos_ref[2], pos_ref[3]
    width = full.shape[1] // 2
    band = left.shape[1]
    owners = other_refs[0].shape[0]
    for k, other_ref in enumerate(other_refs):
        for j in range(2 * width // LANES):
            part_refs = (mine_ref.at[k * owners : (k + 1) * owners], other_ref)
            piece = joined_rows(core, part_refs, j, 0, owners)
            full[k * owners * 16 : (k + 1) * owners * 16, j * LANES : (j + 1) * LANES] = piece
    for k in range(4):

        @pl.when(part == k)
        def _():
            cols = slice(k * band, (k + 1) * band)
            shifted = slice(width + k * band, width + (k + 1) * band)
            left[...] = jnp.where(kind == 0, full[:, cols], full[:, shifted])
            own = pl.ds(pl.multiple_of(owner * 8, 8), 8)
            tile = jnp.where(kind == 0, full[own, cols], full[own, shifted])
            cfg_ref[...] = tile / root_ref[:, :1]

    cross = lax.dot_general(
        left[...],
        full[...],
        (((0,), (0,)), ((), ())),
        precision=lax.Precision.HIGHEST,
        preferred_element_type=jnp.float32,
    )
    cross_ref[...] = cross * (1.0 / full.shape[0])


def final_kernel(norm, pos_ref, mine_ref, other_ref, cross_ref, normal_ref, gram):
    core, kind, part = pos_ref[0], pos_ref[1], pos_ref[2]
    width = gram.shape[1]

    def joined(tile, lo=0, hi=16):
        return joined_rows(core, (mine_ref, other_ref), tile, lo, hi)

    def fill(row, col, piece):
        gram[row : row + piece.shape[0], col : col + piece.shape[1]] = piece

    def straight(tiles, lo, hi, row, col):
        for k, tile in enumerate(tiles):
            fill(row, col + k * LANES, joined(tile, lo, hi))

    def corner():
        return jnp.where(kind == 0, joined(5, 0, 8), joined(5, 8, 16))

    def band_0():
        fill(0, 0, corner())
        fill(128, 0, joined(4, 0, 8).T[:64])
        straight((4, 0, 1, 2, 3), 0, 12, 0, LANES)

    def band_1():
        fill(0, 0, joined(4, 0, 8).T[64:])
        straight((4, 0, 1, 2, 3), 12, 16, 0, LANES)
        fill(64, 0, joined(0).T)
        fill(64, TILE, corner())
        straight((1, 2, 3), 0, 8, 64, TILE + LANES)

    def band_2():
        fill(0, 0, joined(0).T)
        fill(0, TILE, joined(3, 0, 8).T)
        straight((3, 2, 4), 8, 16, 0, TILE + LANES)
        fill(128, 0, joined(1).T[:64])
        fill(128, TILE, joined(2).T[:64])
        fill(128, 2 * TILE, corner()[:64])
        straight((4,), 0, 4, 128, 2 * TILE + LANES)

    def band_3():
        fill(0, 0, joined(0).T[64:])
        fill(64, 0, joined(1).T)
        fill(0, TILE, joined(2).T[64:])
        fill(64, TILE, joined(3).T)
        fill(0, 2 * TILE, corner()[64:])
        fill(64, 2 * TILE, joined(4, 0, 8).T)
        straight((4,), 4, 16, 0, 2 * TILE + LANES)

    for k, body in enumerate((band_0, band_1, band_2, band_3)):
        pl.when(part == k)(body)

    for which in range(2):
        cols = slice(which * width, (which + 1) * width)
        extra = jnp.where(kind == which, gram[...] * (1.0 / norm), 0.0)
        normal_ref[:, cols] = cross_ref[:, cols] + extra


def call(kernel, outs, args, scratch, space, limit, flops):
    smem = pl.BlockSpec(memory_space=pltpu.SMEM)
    held = [pltpu.with_memory_space_constraint(a, space) for a in args[1:]]
    return pl.pallas_call(
        kernel,
        out_shape=outs,
        in_specs=[smem] + [pl.BlockSpec(memory_space=space)] * len(held),
        out_specs=[pl.BlockSpec(memory_space=pltpu.VMEM)] * len(outs),
        scratch_shapes=list(scratch),
        compiler_params=pltpu.CompilerParams(vmem_limit_bytes=limit),
        cost_estimate=pl.CostEstimate(flops=flops, bytes_accessed=flops >> 9, transcendentals=0),
    )(args[0], *held)


def exchange(values, axes):
    flat = values.reshape(-1, values.shape[-1])
    return lax.all_to_all(flat, axes, 0, 0, tiled=True).reshape(values.shape)


def bands_kernel(owner_ref, *refs):
    owner, out_ref = owner_ref[0], refs[-1]
    total = refs[0][...]
    for ref in refs[1:-1]:
        total = total + ref[...]

    def tile(k):
        return total[8 * k : 8 * k + 8]

    def either(first, a, b):
        return jnp.where(owner >= first, tile(a), tile(b))

    bands = (
        [tile(k) for k in (0, 1, 2, 3, 6, 9)],
        [tile(0), either(12, 1, 7), either(12, 2, 4), either(12, 3, 5), tile(6), tile(10)],
        [tile(1), tile(2), tile(4), tile(7), either(8, 5, 8), tile(11)],
        [tile(k) for k in (2, 3, 4, 5, 8, 11)],
    )
    for k in range(16):
        for at, piece in enumerate(bands[k % 4]):
            out_ref[k, at * 8 : at * 8 + 8, :] = piece


def shards(desc, species, atom_cfg, slot, weights):
    atoms, width = desc.shape
    configs = slot.shape[0]
    cfg_here = weights.shape[0]
    n_dev = math.prod(SIZES)
    x, l, core, kind, part = [lax.axis_index(axis) for axis in AXES]
    f32 = jnp.float32

    root = jnp.broadcast_to(jnp.sqrt(weights)[:, None], (cfg_here, LANES))
    pos = jnp.stack([core, kind, part, (x * 4 + l) * 2 + core])

    flip = [(0, 1), (1, 0)]
    int_row = pltpu.VMEM((1, atoms), jnp.int32)
    matrix = pltpu.VMEM((atoms, width), jnp.bfloat16)
    sems = pltpu.SemaphoreType.DMA((6,))

    def tiles(count):
        return pltpu.VMEM((16, count * 8, LANES), f32)

    keep_s, send_s = call(
        sums_kernel,
        [tiles(12)] * 2,
        [core[None], desc, species[None], atom_cfg[None], slot[None]],
        [matrix, int_row, int_row, pltpu.VMEM((1, configs), jnp.int32), sems],
        pltpu.HBM,
        24 << 20,
        4 * configs * atoms * width,
    )
    pair_s, desc, pos, root = lax.optimization_barrier((keep_s + lax.ppermute(send_s, "c", flip), desc, pos, root))
    keep_g, *send_g = call(
        gram_kernel,
        [tiles(21)] + [tiles(6)] * 3 + [tiles(3)],
        [core[None], desc, species[None]],
        [matrix, int_row, pltpu.VMEM((width, atoms), jnp.bfloat16), sems],
        pltpu.HBM,
        24 << 20,
        4 * width * width * atoms,
    )
    pair_g = keep_g + jnp.concatenate([lax.ppermute(part_g, "c", flip) for part_g in send_g], 1)
    plane_s = jnp.sum(exchange(pair_s, ("x", "y")), 0)
    plane_s, pair_g = lax.optimization_barrier((plane_s, pair_g))
    plane_g = jnp.sum(exchange(pair_g, ("x", "y")), 0)

    def along_l(value, k):
        return lax.ppermute(value, "l", [(i, (i + k) % 4) for i in range(4)])

    plane_s = plane_s + lax.ppermute(plane_s, "h", flip)
    rooted = jnp.concatenate([plane_s, root])
    got = [(rooted, l)]
    for k in (1, 3, 2):
        got.append((along_l(rooted, k), (l - k) % 4))
    root_here = sum(jnp.where(source == part, value[96:], 0.0) for value, source in got)
    scale = 1.0 / math.sqrt(atoms * n_dev / configs)
    sums = sum(value[:96] for value, _ in got).reshape(12, 8, LANES) * (root_here * scale)
    sums, plane_g = lax.optimization_barrier((sums, plane_g))
    def of_species(which):
        return jnp.concatenate([lax.dynamic_slice_in_dim(plane_g, which * 72, 72), plane_g[144:]])

    mine_s = exchange(jnp.broadcast_to(sums.reshape(1, 96, LANES), (16, 96, LANES)), ("x", "y"))
    grams = of_species(kind) + lax.ppermute(of_species(1 - kind), "h", flip)
    (spread,) = call(
        bands_kernel,
        [tiles(6)],
        [(x * 4 + part)[None], grams] + [along_l(grams, k) for k in (1, 3, 2)],
        (),
        pltpu.VMEM,
        8 << 20,
        5500000000,
    )
    spread, mine_s = lax.optimization_barrier((spread, mine_s))
    mine_g = exchange(spread, ("x", "y"))
    band = 2 * width // 8
    norm = atoms * n_dev // 8
    cross, rows = call(
        product_kernel,
        [pltpu.VMEM((band, 2 * width), f32), jax.ShapeDtypeStruct((cfg_here, band), f32)],
        [pos, mine_s] + [lax.ppermute(mine_s[k : k + 4], "c", flip) for k in range(0, 16, 4)] + [root],
        [pltpu.VMEM((configs, 2 * width), f32), pltpu.VMEM((configs, band), f32)],
        pltpu.VMEM,
        24 << 20,
        24 * band * width * configs,
    )
    mine_g, cross = lax.optimization_barrier((mine_g, cross))
    (normal,) = call(
        functools.partial(final_kernel, norm),
        [jax.ShapeDtypeStruct((band, 2 * width), f32)],
        [pos, mine_g, lax.ppermute(mine_g, "c", flip), cross],
        [pltpu.VMEM((band, width), f32)],
        pltpu.VMEM,
        24 << 20,
        band * width,
    )
    return normal, rows


def solution(mesh):
    fine = Mesh(mesh.devices.reshape(SIZES), AXES)
    return jax.shard_map(
        shards,
        mesh=fine,
        in_specs=(P(AXES, None), P(AXES), P(AXES), P(), P(("x", "l", "c"))),
        out_specs=(P(("h", "y"), None), P(("x", "l", "c"), ("h", "y"))),
        check_vma=False,
    )
```
